512 devices in a mesh: lon: 128 (over y, x_lo, z), lat: 4 (over x_hi, core).
Axes of the slice: x: 4 (x_hi: 2, x_lo: 2; x = x_hi * 2 + x_lo), y: 4, z: 16, core: 2. Of those that a mesh axis runs over, the one named last changes fastest.
Arguments:
- fields: float32 [64, 2560, 6, 128], P('lat', 'lon'), may hold values from -6 to 6
- day_mask: int32 [2, 64, 2560], P(None, 'lat', 'lon'), may hold values from 0 to 1, as said below
- w_in: bfloat16 [2, 1024, 768], P(None, 'lon'), may hold values from -0.21875 to 0.21875
- w_mid: bfloat16 [2, 1024, 1024], P(None, 'lon'), may hold values from -0.1875 to 0.1875
- w_out: bfloat16 [2, 1024, 768], P(None, 'lon'), may hold values from -0.1875 to 0.1875
Outputs:
- final_fields: float32 [64, 2560, 6, 128], P('lat', 'lon')
The draws below stay inside these ranges and needn't reach their ends.
Inputs may be any that keep to these rules, and one draw needn't show every extreme that they name: day_mask is equal on latitude rows 2 j and 2 j + 1; at longitude index b + 1280 it equals 1 minus its value at longitude b.
All inputs are finite; a program needn't handle non-finite values.
Results may differ from the reference program's by a relative error of at most 0.0075.
Values may be sent and summed in bfloat16 or wider, within the bound.
No kernel may reach another device: no remote copies, remote signals or barrier semaphores. Data moves between devices by JAX's collectives and lax.ppermute only.
A program may use at most 128 MiB of HBM per device.

```python
import jax
import jax.numpy as jnp
from jax import lax

LEV = 128
FIELDS = 6
HIDDEN_SIZE = 1024
STEPS = 2
IN = 768
NLAT = 64
NLON = 2560


def day_pattern(key):
    base_key = jax.random.fold_in(key, 41)
    phase_key, jitter_key = jax.random.split(base_key)
    half_loop = NLON // 2
    spread_cells = max(NLON // 8, 1)
    sun_phase = jax.random.randint(phase_key, (STEPS, 1, 1), 0, NLON)
    jitter = jax.random.randint(jitter_key, (STEPS, NLAT // 2, half_loop), -spread_cells, spread_cells + 1)
    longitude = jnp.arange(half_loop, dtype=jnp.int32)[None, None, :]
    sunlit = (jnp.mod(longitude + jitter - sun_phase, NLON) < half_loop).astype(jnp.int32)
    sunlit = jnp.repeat(sunlit, 2, axis=1)
    return jnp.concatenate([sunlit, 1 - sunlit], axis=2)


def draw_day_mask(key, part):
    return day_pattern(key)


def levels(own_key, shape, shards, least, top_value):
    loudness, own = 1.0, jax.random.fold_in(own_key, 6)
    for position, parts in shards:
        heights = jnp.exp(jax.random.uniform(jax.random.fold_in(own, position), (parts,), jnp.float32, least / len(shards), top_value / len(shards)))
        loudness = loudness * jnp.repeat(heights, shape[position] // parts).reshape([-1 if axis == position else 1 for axis in range(len(shape))])
    return loudness


def scatter_about(stream_key, shape, width, most, shards=(), kind=jnp.bfloat16):
    entries = width * jax.random.normal(stream_key, shape, jnp.float32)
    if shards:
        entries = entries * levels(stream_key, shape, shards, -0.22, 0.18)
    return jnp.clip(entries, -most, most).astype(kind)


def setup_inputs(seed: int = 0) -> dict:
    keys = jax.random.split(jax.random.key(seed), 6)
    return {
        "fields": scatter_about(keys[0], (NLAT, NLON, FIELDS, LEV), 1.0, 6.0, ((0, 4), (1, 128)), jnp.float32),
        "day_mask": draw_day_mask(jax.random.fold_in(keys[5], 71), 0),
        "w_in": scatter_about(keys[2], (2, HIDDEN_SIZE, IN), IN ** -0.5, 0.21875, ((1, 128),)),
        "w_mid": scatter_about(keys[3], (2, HIDDEN_SIZE, HIDDEN_SIZE), HIDDEN_SIZE ** -0.5, 0.1875, ((1, 128),)),
        "w_out": scatter_about(keys[4], (2, HIDDEN_SIZE, IN), HIDDEN_SIZE ** -0.5, 0.1875, ((1, 128),)),
    }


COURANT = 0.25
DIFFUSE = 0.1
EPSILON = 1e-06

def transport(fields_now):
    east_side = jnp.roll(fields_now, -1, axis=1)
    west_side = jnp.roll(fields_now, 1, axis=1)
    zero_row = jnp.zeros_like(fields_now[:1])
    north_side = jnp.concatenate([fields_now[1:], zero_row], axis=0)
    south_side = jnp.concatenate([zero_row, fields_now[:-1]], axis=0)
    wind_east = fields_now[:, :, 0:1]
    wind_north = fields_now[:, :, 1:2]
    advected = wind_east * (east_side - west_side) + wind_north * (north_side - south_side)
    smoothed = east_side + west_side + north_side + south_side - 4.0 * fields_now
    return fields_now - COURANT * advected + DIFFUSE * smoothed

def normalize(columns):
    mean_square = lax.optimization_barrier(jnp.mean(columns * columns, axis=-1, keepdims=True))
    return (columns * lax.rsqrt(mean_square + EPSILON)).astype(jnp.bfloat16)

def network(inputs, first_layer, middle_layer, last_layer):
    before = lax.dot_general(inputs, first_layer, (((1,), (1,)), ((), ())), preferred_element_type=jnp.float32)
    first = jax.nn.silu(before).astype(jnp.bfloat16)
    second = jax.nn.silu(jnp.dot(first, middle_layer, preferred_element_type=jnp.float32)).astype(jnp.bfloat16)
    return jnp.dot(second, last_layer, preferred_element_type=jnp.float32)

def reference(fields, day_mask, w_in, w_mid, w_out):
    fields_now = fields
    for step_index in range(STEPS):
        moved = transport(fields_now)
        rows = moved.reshape(NLAT, NLON, IN)

        def one_latitude(packed):
            columns, sunlit = packed
            inputs = normalize(columns)
            day_output = network(inputs, w_in[0], w_mid[0], w_out[0])
            night_output = network(inputs, w_in[1], w_mid[1], w_out[1])
            return jnp.where(sunlit[:, None] == 1, day_output, night_output)
        tendency = lax.map(one_latitude, (rows, day_mask[step_index]))
        fields_now = moved + tendency.reshape(moved.shape)
    return fields_now
```

```python
import functools

import jax
import jax.numpy as jnp
from jax import lax
from jax.experimental import pallas as pl
from jax.experimental.pallas import tpu as pltpu
from jax.sharding import Mesh
from jax.sharding import PartitionSpec as P

COURANT = 0.25
DIFFUSE = 0.1
EPSILON = 1e-06
AXES = ("y", "xl", "z", "xh", "core")
LON = ("y", "xl", "z")
LAT = ("xh", "core")
F, L = 6, 128
C, R = 20, 16
WIDE = C + 2
MAIN = WIDE * R
ROWS = MAIN + 2 * C + 8
IN = F * L
HID = 1024
HALF = 1280
TILE = 256


def ring_partner(i, kind):
    if kind == 0:
        return i ^ 1
    return (i + 1) % 4 if i % 2 else (i - 1) % 4


def x_exchange(a, rnd):
    pairs = []
    for x in range(4):
        for c in range(2):
            p = ring_partner(x, c if rnd == 0 else 1 - c)
            pairs.append(((x % 2) * 4 + (x // 2) * 2 + c, (p % 2) * 4 + (p // 2) * 2 + c))
    return lax.ppermute(a, ("xl", "xh", "core"), pairs)


def y_exchange(a, rnd):
    pairs = []
    for y in range(4):
        for c in range(2):
            p = ring_partner(y, c if rnd == 0 else 1 - c)
            pairs.append((y * 2 + c, p * 2 + c))
    return lax.ppermute(a, ("y", "core"), pairs)


def core_swap(a):
    return lax.ppermute(a, "core", [(0, 1), (1, 0)])


def gather_weights(block):
    z = lax.all_gather(block, "z", axis=0)
    a, b = z[:8], z[8:]
    a1, b1 = x_exchange(a, 0), y_exchange(b, 0)
    a2, b2 = jnp.stack([a, a1]), jnp.stack([b, b1])
    a3, b3 = x_exchange(a2, 1), y_exchange(b2, 1)
    a4, b4 = jnp.concatenate([a2, a3]), jnp.concatenate([b2, b3])
    a5, b5 = y_exchange(a4, 0), x_exchange(b4, 0)
    a6, b6 = jnp.stack([a4, a5]), jnp.stack([b4, b5])
    a7, b7 = y_exchange(a6, 1), x_exchange(b6, 1)
    ca6, cb6 = core_swap(a6), core_swap(b6)
    ca7, cb7 = core_swap(a7), core_swap(b7)
    return [p.reshape(8 * 64, HALF) for p in (a6, a7, b6, b7, ca6, ca7, cb6, cb7)]


def moved_of(cen, east, west, u, v):
    north = pltpu.roll(cen, cen.shape[0] - 1, 0)
    south = pltpu.roll(cen, 1, 0)
    advected = u * (east - west) + v * (north - south)
    smoothed = east + west + north + south - 4.0 * cen
    return cen - COURANT * advected + DIFFUSE * smoothed


def column_moved(ext, c):
    cen = [ext[c, f] for f in range(F)]
    return [moved_of(cen[f], ext[c + 1, f], ext[c - 1, f], cen[0], cen[1]) for f in range(F)]


def rs_of(parts):
    ss = parts[0] * parts[0]
    for p in parts[1:]:
        ss = ss + p * p
    return lax.rsqrt(jnp.sum(ss, axis=-1, keepdims=True) * (1.0 / IN) + EPSILON)


def lanes(f):
    return slice(f * L, (f + 1) * L)


def prepare_kernel(ft, mask, lon_w, lon_e, lat_s, lat_n, moved, normed, mk, ext, edge):
    moved[MAIN:, :] = jnp.zeros((ROWS - MAIN, IN), jnp.float32)
    mk[MAIN:, :] = jnp.zeros((ROWS - MAIN, L), jnp.float32)

    def own(c, carry):
        for f in range(F):
            ext[c + 2, f, 8 : 8 + R, :] = ft[c, f]
        row = pl.multiple_of((c + 1) * R, R)
        mk[pl.ds(row, R), :] = mask[c]
        return carry

    lax.fori_loop(0, C, own, 0)
    for c in range(2):
        for f in range(F):
            ext[c, f, 8 : 8 + R, :] = lon_w[c, f].astype(jnp.float32)
            ext[C + 2 + c, f, 8 : 8 + R, :] = lon_e[c, f].astype(jnp.float32)
    mk[0:R, :] = lon_w[1, F].astype(jnp.float32)
    mk[MAIN - R : MAIN, :] = lon_e[0, F].astype(jnp.float32)

    def sides(c, carry):
        for f in range(F):
            ext[c + 1, f, 6:8, :] = lat_s[c, f].astype(jnp.float32)
            ext[c + 1, f, 8 + R : 10 + R, :] = lat_n[c, f].astype(jnp.float32)
        return carry

    lax.fori_loop(0, WIDE, sides, 0)

    def step(c, carry):
        parts = column_moved(ext, c + 1)
        rs = rs_of(parts)
        row = pl.multiple_of(c * R, R)
        for f in range(F):
            moved[pl.ds(row, R), lanes(f)] = parts[f][8 : 8 + R]
            normed[pl.ds(row, R), lanes(f)] = (parts[f] * rs)[8 : 8 + R].astype(jnp.bfloat16)

        for f in range(F):
            edge[c, f, 0:1, :] = parts[f][7:8]
            edge[c, f, 1:2, :] = parts[f][8 + R : 9 + R]
        return carry

    lax.fori_loop(0, WIDE, step, 0)
    for c in range(C):
        for k, side in enumerate((lat_s, lat_n)):
            row = MAIN + k * C + c
            for f in range(F):
                moved[row : row + 1, lanes(f)] = edge[c + 1, f, k : k + 1, :]
            mk[row : row + 1, :] = side[c + 1, F].astype(jnp.float32)[1 - k : 2 - k]
    tail = [moved[MAIN:, lanes(f)] for f in range(F)]
    rs = rs_of(tail)
    for f in range(F):
        normed[MAIN:, lanes(f)] = (tail[f] * rs).astype(jnp.bfloat16)


def silu(t):
    half = 0.5 * t
    return (half + half * jnp.tanh(half)).astype(jnp.bfloat16)


def networks(x, mask_ref, weights, h1, h2, out, rows):
    def net(n, carry):
        want = (1 - n).astype(jnp.float32)
        for t in range(HID // TILE):
            w = weights[n, t * TILE : (t + 1) * TILE, 0:IN]
            d = lax.dot_general(x[...], w, (((1,), (1,)), ((), ())), preferred_element_type=jnp.float32)
            h1[0:rows, t * TILE : (t + 1) * TILE] = silu(d)
        for t in range(HID // TILE):
            w = weights[n, :, IN + t * TILE : IN + (t + 1) * TILE]
            d = jnp.dot(h1[0:rows, :], w, preferred_element_type=jnp.float32)
            h2[0:rows, t * TILE : (t + 1) * TILE] = silu(d)
        pick = mask_ref[...] == want
        pick = jnp.concatenate([pick, pick], axis=1)
        for t in range(IN // TILE):
            cols = slice(t * TILE, (t + 1) * TILE)
            w = weights[n, :, IN + HID + t * TILE : IN + HID + (t + 1) * TILE]
            d = jnp.dot(h2[0:rows, :], w, preferred_element_type=jnp.float32)
            out[0:rows, cols] = jnp.where(pick, d, out[0:rows, cols])
        return carry

    lax.fori_loop(0, 2, net, 0)


def step_kernel(table, x1, moved1, mask0, mask1, *rest):
    pieces = rest[:8]
    result = rest[8]
    weights, h1, h2, out, ext, x2, moved2, sems = rest[9:]
    core = table[16]
    copies = []
    for k in range(8):
        net = core if k < 4 else 1 - core
        colour = (k // 2) % 2
        late = (k % 2) * 2
        for p in range(2):
            for q in range(4):
                j, i = (late + p, q) if colour == 0 else (q, late + p)
                x = table[net * 8 + i]
                y = table[net * 8 + 4 + j]
                row = pl.multiple_of(y * 256 + (x % 2) * 128 + colour * 64, 64)
                col = pl.multiple_of((x // 2) * HALF, 128)
                src = pieces[k].at[pl.ds((p * 4 + q) * 64, 64), :]
                dst = weights.at[net, pl.ds(row, 64), pl.ds(col, HALF)]
                copies.append(pltpu.make_async_copy(src, dst, sems.at[len(copies)]))
    for c in copies:
        c.start()
    for c in copies:
        c.wait()

    networks(x1, mask0, weights, h1, h2, out, ROWS)

    def spread(c, carry):
        row = pl.multiple_of(c * R, R)
        for f in range(F):
            ext[c, f, 8 : 8 + R, :] = moved1[pl.ds(row, R), lanes(f)] + out[pl.ds(row, R), lanes(f)]
        return carry

    lax.fori_loop(0, WIDE, spread, 0)

    for c in range(C):
        for k, (at, flag) in enumerate(((7, 17), (8 + R, 18))):
            row = MAIN + k * C + c
            value = moved1[row : row + 1, :] + out[row : row + 1, :]
            value = jnp.where(table[flag] == 1, value, jnp.zeros_like(value))
            for f in range(F):
                ext[c + 1, f, at : at + 1, :] = value[:, lanes(f)]

    def second(c, carry):
        parts = column_moved(ext, c + 1)
        rs = rs_of(parts)
        row = pl.multiple_of(c * R, R)
        for f in range(F):
            moved2[pl.ds(row, R), lanes(f)] = parts[f][8 : 8 + R]
            x2[pl.ds(row, R), lanes(f)] = (parts[f] * rs)[8 : 8 + R].astype(jnp.bfloat16)
        return carry

    lax.fori_loop(0, C, second, 0)
    networks(x2, mask1, weights, h1, h2, out, C * R)

    def finish(c, carry):
        row = pl.multiple_of(c * R, R)
        for f in range(F):
            result[c, f] = moved2[pl.ds(row, R), lanes(f)] + out[pl.ds(row, R), lanes(f)]
        return carry

    lax.fori_loop(0, C, finish, 0)


def vmem(n):
    return [pl.BlockSpec(memory_space=pltpu.VMEM)] * n


def shards(fields, day_mask, w_in, w_mid, w_out):
    y, xl, xh, core = (lax.axis_index(a) for a in ("y", "xl", "xh", "core"))
    lat = xh * 2 + core

    joined = jnp.concatenate([w_in, w_mid, w_out], axis=2)
    block = lax.dynamic_slice(joined, (core, 0, xh * HALF), (1, 8, HALF))[0]
    pieces = gather_weights(block)

    ft = fields.transpose(1, 2, 0, 3)
    masks = jnp.broadcast_to(
        day_mask.transpose(0, 2, 1)[..., None].astype(jnp.float32), (2, C, R, L)
    )
    both = jnp.concatenate([ft.astype(jnp.bfloat16), masks[0][:, None].astype(jnp.bfloat16)], axis=1)
    lon_n = 128
    lon_w = lax.ppermute(both[C - 2 :], LON, [(i, (i + 1) % lon_n) for i in range(lon_n)])
    lon_e = lax.ppermute(both[:2], LON, [((i + 1) % lon_n, i) for i in range(lon_n)])
    wide = jnp.concatenate([lon_w[1:], both, lon_e[:1]], axis=0)
    lat_s = lax.ppermute(wide[:, :, R - 2 :], LAT, [(i, i + 1) for i in range(3)])
    lat_n = lax.ppermute(wide[:, :, :2], LAT, [(i + 1, i) for i in range(3)])

    moved1, x1, mask0 = pl.pallas_call(
        prepare_kernel,
        out_shape=(
            jax.ShapeDtypeStruct((ROWS, IN), jnp.float32),
            jax.ShapeDtypeStruct((ROWS, IN), jnp.bfloat16),
            jax.ShapeDtypeStruct((ROWS, L), jnp.float32),
        ),
        in_specs=vmem(6),
        out_specs=vmem(3),
        scratch_shapes=[
            pltpu.VMEM((C + 4, F, 32, L), jnp.float32),
            pltpu.VMEM((WIDE, F, 8, L), jnp.float32),
        ],
        compiler_params=pltpu.CompilerParams(vmem_limit_bytes=12 << 20),
        name="prepare",
    )(ft, masks[0], lon_w, lon_e, lat_s, lat_n)

    x = xh * 2 + xl

    def partners(i):
        return i ^ 1, jnp.where(i % 2 == 1, (i + 1) % 4, (i + 3) % 4)

    def order(i, net):
        p, n = partners(i)[net], partners(i)[1 - net]
        return [i, p, n, partners(n)[net]]

    entries = [*order(x, 0), *order(y, 0), *order(x, 1), *order(y, 1)]
    entries += [core, (lat > 0).astype(jnp.int32), (lat < 3).astype(jnp.int32)]
    table = jnp.stack([e.astype(jnp.int32) for e in entries])

    result = pl.pallas_call(
        step_kernel,
        out_shape=jax.ShapeDtypeStruct((C, F, R, L), jnp.float32),
        in_specs=[pl.BlockSpec(memory_space=pltpu.SMEM)]
        + vmem(4)
        + [pl.BlockSpec(memory_space=pl.ANY)] * 8,
        out_specs=pl.BlockSpec(memory_space=pltpu.VMEM),
        scratch_shapes=[
            pltpu.VMEM((2, HID, 2 * HALF), jnp.bfloat16),
            pltpu.VMEM((ROWS, HID), jnp.bfloat16),
            pltpu.VMEM((ROWS, HID), jnp.bfloat16),
            pltpu.VMEM((ROWS, IN), jnp.float32),
            pltpu.VMEM((WIDE, F, 32, L), jnp.float32),
            pltpu.VMEM((C * R, IN), jnp.bfloat16),
            pltpu.VMEM((C * R, IN), jnp.float32),
            pltpu.SemaphoreType.DMA((64,)),
        ],
        compiler_params=pltpu.CompilerParams(vmem_limit_bytes=36 << 20),
        name="steps",
    )(table, x1, moved1, mask0, masks[1].reshape(C * R, L), *pieces)
    return result.transpose(2, 0, 1, 3)


def solution(mesh):
    grid = Mesh(mesh.devices.reshape(4, 2, 16, 2, 2), AXES)
    in_specs = (
        P(LAT, LON, None, None),
        P(None, LAT, LON),
        P(None, LON, None),
        P(None, LON, None),
        P(None, LON, None),
    )
    return jax.shard_map(
        shards, mesh=grid, in_specs=in_specs, out_specs=P(LAT, LON, None, None), check_vma=False
    )
```

```python
import jax
import jax.numpy as jnp
import numpy as np
from jax import lax
from jax.experimental import pallas as pl
from jax.experimental.pallas import tpu as pltpu
from jax.sharding import Mesh
from jax.sharding import PartitionSpec as P

COURANT = 0.25
DIFFUSE = 0.1
EPSILON = 1e-06
AXES = ("y", "xl", "z", "xh", "core")
LON = ("y", "xl", "z")
LAT = ("xh", "core")
F, L = 6, 128
C, R = 20, 16
WIDE = C + 2
MAIN = WIDE * R
ROWS = MAIN + 2 * C + 8
IN = F * L
HID = 1024
HALF = 1280
TILE = 256


def ring_partner(i, kind):
    if kind == 0:
        return i ^ 1
    return (i + 1) % 4 if i % 2 else (i - 1) % 4


def x_exchange(a, rnd):
    pairs = []
    for x in range(4):
        for c in range(2):
            p = ring_partner(x, c if rnd == 0 else 1 - c)
            pairs.append(((x % 2) * 4 + (x // 2) * 2 + c, (p % 2) * 4 + (p // 2) * 2 + c))
    return lax.ppermute(a, ("xl", "xh", "core"), pairs)


def y_exchange(a, rnd):
    pairs = []
    for y in range(4):
        for c in range(2):
            p = ring_partner(y, c if rnd == 0 else 1 - c)
            pairs.append((y * 2 + c, p * 2 + c))
    return lax.ppermute(a, ("y", "core"), pairs)


def core_swap(a):
    return lax.ppermute(a, "core", [(0, 1), (1, 0)])


def gather_weights(block):
    z = lax.all_gather(block, "z", axis=0)
    a, b = z[:8], z[8:]
    a1, b1 = x_exchange(a, 0), y_exchange(b, 0)
    a2, b2 = jnp.stack([a, a1]), jnp.stack([b, b1])
    a3, b3 = x_exchange(a2, 1), y_exchange(b2, 1)
    a4, b4 = jnp.concatenate([a2, a3]), jnp.concatenate([b2, b3])
    a5, b5 = y_exchange(a4, 0), x_exchange(b4, 0)
    a6, b6 = jnp.stack([a4, a5]), jnp.stack([b4, b5])
    a7, b7 = y_exchange(a6, 1), x_exchange(b6, 1)
    ca6, cb6 = core_swap(a6), core_swap(b6)
    ca7, cb7 = core_swap(a7), core_swap(b7)
    return [p.reshape(8 * 64, HALF) for p in (a6, a7, b6, b7, ca6, ca7, cb6, cb7)]


def moved_of(cen, east, west, u, v):
    north = pltpu.roll(cen, cen.shape[0] - 1, 0)
    south = pltpu.roll(cen, 1, 0)
    advected = u * (east - west) + v * (north - south)
    smoothed = east + west + north + south - 4.0 * cen
    return cen - COURANT * advected + DIFFUSE * smoothed


def column_moved(ext, c):
    cen = [ext[c, f] for f in range(F)]
    return [moved_of(cen[f], ext[c + 1, f], ext[c - 1, f], cen[0], cen[1]) for f in range(F)]


def rs_of(parts):
    ss = parts[0] * parts[0]
    for p in parts[1:]:
        ss = ss + p * p
    return lax.rsqrt(jnp.sum(ss, axis=-1, keepdims=True) * (1.0 / IN) + EPSILON)


def lanes(f):
    return slice(f * L, (f + 1) * L)


def prepare_kernel(ft, mask, lon_w, lon_e, lat_s, lat_n, moved, normed, mk, ext, edge):
    moved[MAIN:, :] = jnp.zeros((ROWS - MAIN, IN), jnp.float32)
    mk[MAIN:, :] = jnp.zeros((ROWS - MAIN, L), jnp.float32)

    def own(c, carry):
        for f in range(F):
            ext[c + 2, f, 8 : 8 + R, :] = ft[c, f]
        row = pl.multiple_of((c + 1) * R, R)
        mk[pl.ds(row, R), :] = mask[c]
        return carry

    lax.fori_loop(0, C, own, 0)
    for c in range(2):
        for f in range(F):
            ext[c, f, 8 : 8 + R, :] = lon_w[c, f].astype(jnp.float32)
            ext[C + 2 + c, f, 8 : 8 + R, :] = lon_e[c, f].astype(jnp.float32)
    mk[0:R, :] = lon_w[1, F].astype(jnp.float32)
    mk[MAIN - R : MAIN, :] = lon_e[0, F].astype(jnp.float32)

    def sides(c, carry):
        for f in range(F):
            ext[c + 1, f, 6:8, :] = lat_s[c, f].astype(jnp.float32)
            ext[c + 1, f, 8 + R : 10 + R, :] = lat_n[c, f].astype(jnp.float32)
        return carry

    lax.fori_loop(0, WIDE, sides, 0)

    def step(c, carry):
        parts = column_moved(ext, c + 1)
        rs = rs_of(parts)
        row = pl.multiple_of(c * R, R)
        for f in range(F):
            moved[pl.ds(row, R), lanes(f)] = parts[f][8 : 8 + R]
            normed[pl.ds(row, R), lanes(f)] = (parts[f] * rs)[8 : 8 + R].astype(jnp.bfloat16)

        for f in range(F):
            edge[c, f, 0:1, :] = parts[f][7:8]
            edge[c, f, 1:2, :] = parts[f][8 + R : 9 + R]
        return carry

    lax.fori_loop(0, WIDE, step, 0)
    for c in range(C):
        for k, side in enumerate((lat_s, lat_n)):
            row = MAIN + k * C + c
            for f in range(F):
                moved[row : row + 1, lanes(f)] = edge[c + 1, f, k : k + 1, :]
            mk[row : row + 1, :] = side[c + 1, F].astype(jnp.float32)[1 - k : 2 - k]
    tail = [moved[MAIN:, lanes(f)] for f in range(F)]
    rs = rs_of(tail)
    for f in range(F):
        normed[MAIN:, lanes(f)] = (tail[f] * rs).astype(jnp.bfloat16)


def silu(t):
    half = 0.5 * t
    return (half + half * jnp.tanh(half)).astype(jnp.bfloat16)


def networks(x, mask_ref, weights, h1, h2, out, rows, arrive):
    def net(n, carry):
        if arrive:
            arrive(n, 0)
        want = (1 - n).astype(jnp.float32)
        for t in range(HID // TILE):
            w = weights[n, t * TILE : (t + 1) * TILE, 0:IN]
            d = lax.dot_general(x[...], w, (((1,), (1,)), ((), ())), preferred_element_type=jnp.float32)
            h1[0:rows, t * TILE : (t + 1) * TILE] = silu(d)
        if arrive:
            arrive(n, 1)
        for t in range(HID // TILE):
            w = weights[n, :, IN + t * TILE : IN + (t + 1) * TILE]
            d = jnp.dot(h1[0:rows, :], w, preferred_element_type=jnp.float32)
            h2[0:rows, t * TILE : (t + 1) * TILE] = silu(d)
        pick = mask_ref[...] == want
        pick = jnp.concatenate([pick, pick], axis=1)
        for t in range(IN // TILE):
            cols = slice(t * TILE, (t + 1) * TILE)
            w = weights[n, :, IN + HID + t * TILE : IN + HID + (t + 1) * TILE]
            d = jnp.dot(h2[0:rows, :], w, preferred_element_type=jnp.float32)
            out[0:rows, cols] = jnp.where(pick, d, out[0:rows, cols])
        return carry

    lax.fori_loop(0, 2, net, 0)


def step_kernel(table, x1, moved1, mask0, mask1, *rest):
    pieces = rest[:8]
    result = rest[8]
    weights, h1, h2, out, ext, x2, moved2, sems = rest[9:]
    core = table[16]
    for k in range(8):
        net = core if k < 4 else 1 - core
        colour = (k // 2) % 2
        late = (k % 2) * 2
        for p in range(2):
            for q in range(4):
                j, i = (late + p, q) if colour == 0 else (q, late + p)
                x = table[net * 8 + i]
                y = table[net * 8 + 4 + j]
                row = pl.multiple_of(y * 256 + (x % 2) * 128 + colour * 64, 64)
                col = pl.multiple_of((x // 2) * HALF, 128)
                src = pieces[k].at[pl.ds((p * 4 + q) * 64, 64), :]
                dst = weights.at[net, pl.ds(row, 64), pl.ds(col, HALF)]
                sem = (net * 2 + x // 2) * 16 + y * 4 + (x % 2) * 2 + colour
                pltpu.make_async_copy(src, dst, sems.at[sem]).start()

    def arrive(net, half):
        for k in range(16):
            src = pieces[0].at[pl.ds(0, 64), :]
            dst = weights.at[net, pl.ds(k * 64, 64), pl.ds(half * HALF, HALF)]
            pltpu.make_async_copy(src, dst, sems.at[(net * 2 + half) * 16 + k]).wait()

    networks(x1, mask0, weights, h1, h2, out, ROWS, arrive)

    def spread(c, carry):
        row = pl.multiple_of(c * R, R)
        for f in range(F):
            ext[c, f, 8 : 8 + R, :] = moved1[pl.ds(row, R), lanes(f)] + out[pl.ds(row, R), lanes(f)]
        return carry

    lax.fori_loop(0, WIDE, spread, 0)

    for c in range(C):
        for k, (at, flag) in enumerate(((7, 17), (8 + R, 18))):
            row = MAIN + k * C + c
            value = moved1[row : row + 1, :] + out[row : row + 1, :]
            value = jnp.where(table[flag] == 1, value, jnp.zeros_like(value))
            for f in range(F):
                ext[c + 1, f, at : at + 1, :] = value[:, lanes(f)]

    def second(c, carry):
        parts = column_moved(ext, c + 1)
        rs = rs_of(parts)
        row = pl.multiple_of(c * R, R)
        for f in range(F):
            moved2[pl.ds(row, R), lanes(f)] = parts[f][8 : 8 + R]
            x2[pl.ds(row, R), lanes(f)] = (parts[f] * rs)[8 : 8 + R].astype(jnp.bfloat16)
        return carry

    lax.fori_loop(0, C, second, 0)
    networks(x2, mask1, weights, h1, h2, out, C * R, None)

    def finish(c, carry):
        row = pl.multiple_of(c * R, R)
        for f in range(F):
            result[c, f] = moved2[pl.ds(row, R), lanes(f)] + out[pl.ds(row, R), lanes(f)]
        return carry

    lax.fori_loop(0, C, finish, 0)


def position_table():
    out = np.zeros((32, 32), np.int32)

    def order(i, net):
        p = ring_partner(i, net)
        n = ring_partner(i, 1 - net)
        return [i, p, n, ring_partner(n, net)]

    for y, xl, xh, core in np.ndindex(4, 2, 2, 2):
        x, lat = xh * 2 + xl, xh * 2 + core
        row = order(x, 0) + order(y, 0) + order(x, 1) + order(y, 1) + [core, int(lat > 0), int(lat < 3)]
        out[((y * 2 + xl) * 2 + xh) * 2 + core, : len(row)] = row
    return out


def vmem(n):
    return [pl.BlockSpec(memory_space=pltpu.VMEM)] * n


def shards(fields, day_mask, w_in, w_mid, w_out):
    y, xl, xh, core = (lax.axis_index(a) for a in ("y", "xl", "xh", "core"))
    joined = jnp.concatenate([w_in, w_mid, w_out], axis=2)
    block = lax.dynamic_slice(joined, (core, 0, xh * HALF), (1, 8, HALF))[0]
    pieces = gather_weights(block)

    ft = fields.transpose(1, 2, 0, 3)
    masks = jnp.broadcast_to(
        day_mask.transpose(0, 2, 1)[..., None].astype(jnp.float32), (2, C, R, L)
    )
    lon_n, lat_n_blocks = 128, 4

    def packed(cols, rows):
        part = ft[cols, :, rows].astype(jnp.bfloat16)
        return jnp.concatenate([part, masks[0][cols, None, rows].astype(jnp.bfloat16)], axis=1)

    lon_w = lax.ppermute(
        packed(slice(C - 2, C), slice(0, R)), LON, [(i, (i + 1) % lon_n) for i in range(lon_n)]
    )
    lon_e = lax.ppermute(
        packed(slice(0, 2), slice(0, R)), LON, [((i + 1) % lon_n, i) for i in range(lon_n)]
    )

    def wide(rows):
        return jnp.concatenate(
            [lon_w[1:, :, rows], packed(slice(0, C), rows), lon_e[:1, :, rows]], axis=0
        )

    ends = range(lat_n_blocks - 1)
    lat_s = lax.ppermute(wide(slice(R - 2, R)), LAT, [(i, i + 1) for i in ends])
    lat_n = lax.ppermute(wide(slice(0, 2)), LAT, [(i + 1, i) for i in ends])

    prepare = pl.pallas_call(
        prepare_kernel,
        out_shape=(
            jax.ShapeDtypeStruct((ROWS, IN), jnp.float32),
            jax.ShapeDtypeStruct((ROWS, IN), jnp.bfloat16),
            jax.ShapeDtypeStruct((ROWS, L), jnp.float32),
        ),
        in_specs=vmem(6),
        out_specs=vmem(3),
        scratch_shapes=[
            pltpu.VMEM((C + 4, F, 32, L), jnp.float32),
            pltpu.VMEM((WIDE, F, 8, L), jnp.float32),
        ],
        compiler_params=pltpu.CompilerParams(vmem_limit_bytes=12 << 20),
        name="prepare",
    )
    moved1, x1, mask0 = prepare(ft, masks[0], lon_w, lon_e, lat_s, lat_n)

    at = ((y * 2 + xl) * 2 + xh) * 2 + core
    table = lax.dynamic_slice(jnp.asarray(position_table()), (at, 0), (1, 32))[0]

    result = pl.pallas_call(
        step_kernel,
        out_shape=jax.ShapeDtypeStruct((C, F, R, L), jnp.float32),
        in_specs=[pl.BlockSpec(memory_space=pltpu.SMEM)]
        + vmem(4)
        + [pl.BlockSpec(memory_space=pl.ANY)] * 8,
        out_specs=pl.BlockSpec(memory_space=pltpu.VMEM),
        scratch_shapes=[
            pltpu.VMEM((2, HID, 2 * HALF), jnp.bfloat16),
            pltpu.VMEM((ROWS, HID), jnp.bfloat16),
            pltpu.VMEM((ROWS, HID), jnp.bfloat16),
            pltpu.VMEM((ROWS, IN), jnp.float32),
            pltpu.VMEM((WIDE, F, 32, L), jnp.float32),
            pltpu.VMEM((C * R, IN), jnp.bfloat16),
            pltpu.VMEM((C * R, IN), jnp.float32),
            pltpu.SemaphoreType.DMA((64,)),
        ],
        compiler_params=pltpu.CompilerParams(vmem_limit_bytes=36 << 20),
        name="steps",
    )(table, x1, moved1, mask0, masks[1].reshape(C * R, L), *pieces)
    return result.transpose(2, 0, 1, 3)


def solution(mesh):
    grid = Mesh(mesh.devices.reshape(4, 2, 16, 2, 2), AXES)
    in_specs = (
        P(LAT, LON, None, None),
        P(None, LAT, LON),
        P(None, LON, None),
        P(None, LON, None),
        P(None, LON, None),
    )

    return jax.shard_map(
        shards, mesh=grid, in_specs=in_specs, out_specs=P(LAT, LON, None, None), check_vma=False
    )
```

```python
import jax
import jax.numpy as jnp
import numpy as np
from jax import lax
from jax.experimental import pallas as pl
from jax.experimental.pallas import tpu as pltpu
from jax.sharding import Mesh
from jax.sharding import PartitionSpec as P

COURANT = 0.25
DIFFUSE = 0.1
EPSILON = 1e-06
AXES = ("y", "xl", "z", "xh", "core")
LON = ("y", "xl", "z")
LAT = ("xh", "core")
F, L = 6, 128
C, R = 20, 16
WIDE = C + 2
MAIN = WIDE * R
ROWS = MAIN + 2 * C + 8
IN = F * L
HID = 1024
HALF = 1280
TILE = 256


def ring_partner(i, kind):
    if kind == 0:
        return i ^ 1
    return (i + 1) % 4 if i % 2 else (i - 1) % 4


def x_exchange(a, rnd):
    pairs = []
    for x in range(4):
        for c in range(2):
            p = ring_partner(x, c if rnd == 0 else 1 - c)
            pairs.append(((x % 2) * 4 + (x // 2) * 2 + c, (p % 2) * 4 + (p // 2) * 2 + c))
    return lax.ppermute(a, ("xl", "xh", "core"), pairs)


def y_exchange(a, rnd):
    pairs = []
    for y in range(4):
        for c in range(2):
            p = ring_partner(y, c if rnd == 0 else 1 - c)
            pairs.append((y * 2 + c, p * 2 + c))
    return lax.ppermute(a, ("y", "core"), pairs)


def core_swap(a):
    return lax.ppermute(a, "core", [(0, 1), (1, 0)])


def gather_weights(block):
    z = lax.all_gather(block, "z", axis=0)
    a, b = z[:8], z[8:]
    a1, b1 = x_exchange(a, 0), y_exchange(b, 0)
    a2, b2 = jnp.stack([a, a1]), jnp.stack([b, b1])
    a3, b3 = x_exchange(a2, 1), y_exchange(b2, 1)
    a4, b4 = jnp.concatenate([a2, a3]), jnp.concatenate([b2, b3])
    a5, b5 = y_exchange(a4, 0), x_exchange(b4, 0)
    a6, b6 = jnp.stack([a4, a5]), jnp.stack([b4, b5])
    a7, b7 = y_exchange(a6, 1), x_exchange(b6, 1)
    ca6, cb6 = core_swap(a6), core_swap(b6)
    ca7, cb7 = core_swap(a7), core_swap(b7)
    return [p.reshape(8 * 64, HALF) for p in (a6, a7, b6, b7, ca6, ca7, cb6, cb7)]


def moved_of(cen, east, west, u, v):
    north = pltpu.roll(cen, cen.shape[0] - 1, 0)
    south = pltpu.roll(cen, 1, 0)
    advected = u * (east - west) + v * (north - south)
    smoothed = east + west + north + south - 4.0 * cen
    return cen - COURANT * advected + DIFFUSE * smoothed


def column_moved(ext, c):
    cen = [ext[c, f] for f in range(F)]
    return [moved_of(cen[f], ext[c + 1, f], ext[c - 1, f], cen[0], cen[1]) for f in range(F)]


def rs_of(parts):
    ss = parts[0] * parts[0]
    for p in parts[1:]:
        ss = ss + p * p
    return lax.rsqrt(jnp.sum(ss, axis=-1, keepdims=True) * (1.0 / IN) + EPSILON)


def lanes(f):
    return slice(f * L, (f + 1) * L)


def prepare_kernel(ft, mask, lon_w, lon_e, lat_s, lat_n, moved, normed, mk, ext, edge):
    moved[MAIN:, :] = jnp.zeros((ROWS - MAIN, IN), jnp.float32)
    mk[MAIN:, :] = jnp.zeros((ROWS - MAIN, L), jnp.float32)

    def own(c, carry):
        for f in range(F):
            ext[c + 2, f, 8 : 8 + R, :] = ft[c, f]
        row = pl.multiple_of((c + 1) * R, R)
        mk[pl.ds(row, R), :] = mask[c]
        return carry

    lax.fori_loop(0, C, own, 0)
    for c in range(2):
        for f in range(F):
            ext[c, f, 8 : 8 + R, :] = lon_w[c, f].astype(jnp.float32)
            ext[C + 2 + c, f, 8 : 8 + R, :] = lon_e[c, f].astype(jnp.float32)
    mk[0:R, :] = lon_w[1, F].astype(jnp.float32)
    mk[MAIN - R : MAIN, :] = lon_e[0, F].astype(jnp.float32)

    def sides(c, carry):
        for f in range(F):
            ext[c + 1, f, 6:8, :] = lat_s[c, f].astype(jnp.float32)
            ext[c + 1, f, 8 + R : 10 + R, :] = lat_n[c, f].astype(jnp.float32)
        return carry

    lax.fori_loop(0, WIDE, sides, 0)

    def step(c, carry):
        parts = column_moved(ext, c + 1)
        rs = rs_of(parts)
        row = pl.multiple_of(c * R, R)
        for f in range(F):
            moved[pl.ds(row, R), lanes(f)] = parts[f][8 : 8 + R]
            normed[pl.ds(row, R), lanes(f)] = (parts[f] * rs)[8 : 8 + R].astype(jnp.bfloat16)

        for f in range(F):
            edge[c, f, 0:1, :] = parts[f][7:8]
            edge[c, f, 1:2, :] = parts[f][8 + R : 9 + R]
        return carry

    lax.fori_loop(0, WIDE, step, 0)
    for c in range(C):
        for k, side in enumerate((lat_s, lat_n)):
            row = MAIN + k * C + c
            for f in range(F):
                moved[row : row + 1, lanes(f)] = edge[c + 1, f, k : k + 1, :]
            mk[row : row + 1, :] = side[c + 1, F].astype(jnp.float32)[1 - k : 2 - k]
    tail = [moved[MAIN:, lanes(f)] for f in range(F)]
    rs = rs_of(tail)
    for f in range(F):
        normed[MAIN:, lanes(f)] = (tail[f] * rs).astype(jnp.bfloat16)


def silu(t):
    half = 0.5 * t
    return (half + half * jnp.tanh(half)).astype(jnp.bfloat16)


def networks(x, mask_ref, weights, h1, h2, out, rows, arrive):
    def net(n, carry):
        if arrive:
            arrive(n, 0)
        want = (1 - n).astype(jnp.float32)
        for t in range(HID // TILE):
            w = weights[n, t * TILE : (t + 1) * TILE, 0:IN]
            d = lax.dot_general(x[...], w, (((1,), (1,)), ((), ())), preferred_element_type=jnp.float32)
            h1[0:rows, t * TILE : (t + 1) * TILE] = silu(d)
        if arrive:
            arrive(n, 1)
        for t in range(HID // TILE):
            w = weights[n, :, IN + t * TILE : IN + (t + 1) * TILE]
            d = jnp.dot(h1[0:rows, :], w, preferred_element_type=jnp.float32)
            h2[0:rows, t * TILE : (t + 1) * TILE] = silu(d)
        pick = mask_ref[...] == want
        pick = jnp.concatenate([pick, pick], axis=1)
        for t in range(IN // TILE):
            cols = slice(t * TILE, (t + 1) * TILE)
            w = weights[n, :, IN + HID + t * TILE : IN + HID + (t + 1) * TILE]
            d = jnp.dot(h2[0:rows, :], w, preferred_element_type=jnp.float32)
            out[0:rows, cols] = jnp.where(pick, d, out[0:rows, cols])
        return carry

    lax.fori_loop(0, 2, net, 0)


def step_kernel(table, x1, moved1, mask0, mask1, *rest):
    pieces = rest[:8]
    result = rest[8]
    weights, h1, h2, out, ext, x2, moved2, sems = rest[9:]
    core = table[16]
    for k in range(8):
        net = core if k < 4 else 1 - core
        colour = (k // 2) % 2
        late = (k % 2) * 2
        for p in range(2):
            for q in range(4):
                j, i = (late + p, q) if colour == 0 else (q, late + p)
                x = table[net * 8 + i]
                y = table[net * 8 + 4 + j]
                row = pl.multiple_of(y * 256 + (x % 2) * 128 + colour * 64, 64)
                col = pl.multiple_of((x // 2) * HALF, 128)
                src = pieces[k].at[pl.ds((p * 4 + q) * 64, 64), :]
                dst = weights.at[net, pl.ds(row, 64), pl.ds(col, HALF)]
                sem = (net * 2 + x // 2) * 16 + y * 4 + (x % 2) * 2 + colour
                pltpu.make_async_copy(src, dst, sems.at[sem]).start()

    def arrive(net, half):
        for k in range(16):
            src = pieces[0].at[pl.ds(0, 64), :]
            dst = weights.at[net, pl.ds(k * 64, 64), pl.ds(half * HALF, HALF)]
            pltpu.make_async_copy(src, dst, sems.at[(net * 2 + half) * 16 + k]).wait()

    networks(x1, mask0, weights, h1, h2, out, ROWS, arrive)

    def spread(c, carry):
        row = pl.multiple_of(c * R, R)
        for f in range(F):
            ext[c, f, 8 : 8 + R, :] = moved1[pl.ds(row, R), lanes(f)] + out[pl.ds(row, R), lanes(f)]
        return carry

    lax.fori_loop(0, WIDE, spread, 0)

    for c in range(C):
        for k, (at, flag) in enumerate(((7, 17), (8 + R, 18))):
            row = MAIN + k * C + c
            value = moved1[row : row + 1, :] + out[row : row + 1, :]
            value = jnp.where(table[flag] == 1, value, jnp.zeros_like(value))
            for f in range(F):
                ext[c + 1, f, at : at + 1, :] = value[:, lanes(f)]

    def second(c, carry):
        parts = column_moved(ext, c + 1)
        rs = rs_of(parts)
        row = pl.multiple_of(c * R, R)
        for f in range(F):
            moved2[pl.ds(row, R), lanes(f)] = parts[f][8 : 8 + R]
            x2[pl.ds(row, R), lanes(f)] = (parts[f] * rs)[8 : 8 + R].astype(jnp.bfloat16)
        return carry

    lax.fori_loop(0, C, second, 0)
    networks(x2, mask1, weights, h1, h2, out, C * R, None)

    def finish(c, carry):
        row = pl.multiple_of(c * R, R)
        for f in range(F):
            result[c, f] = moved2[pl.ds(row, R), lanes(f)] + out[pl.ds(row, R), lanes(f)]
        return carry

    lax.fori_loop(0, C, finish, 0)


def position_table():
    out = np.zeros((32, 32), np.int32)

    def order(i, net):
        p = ring_partner(i, net)
        n = ring_partner(i, 1 - net)
        return [i, p, n, ring_partner(n, net)]

    for y, xl, xh, core in np.ndindex(4, 2, 2, 2):
        x, lat = xh * 2 + xl, xh * 2 + core
        row = order(x, 0) + order(y, 0) + order(x, 1) + order(y, 1) + [core, int(lat > 0), int(lat < 3)]
        out[((y * 2 + xl) * 2 + xh) * 2 + core, : len(row)] = row
    return out


def vmem(n):
    return [pl.BlockSpec(memory_space=pltpu.VMEM)] * n


def shards(fields, day_mask, w_in, w_mid, w_out):
    y, xl, xh, core = (lax.axis_index(a) for a in ("y", "xl", "xh", "core"))
    at = ((y * 2 + xl) * 2 + xh) * 2 + core
    table = lax.dynamic_slice(jnp.asarray(position_table()), (at, 0), (1, 32))[0]

    joined = jnp.concatenate([w_in, w_mid, w_out], axis=2)
    block = lax.dynamic_slice(joined, (core, 0, xh * HALF), (1, 8, HALF))[0]
    block, table = lax.optimization_barrier((block, table))
    pieces = gather_weights(block)

    ft = fields.transpose(1, 2, 0, 3)
    masks = jnp.broadcast_to(
        day_mask.transpose(0, 2, 1)[..., None].astype(jnp.float32), (2, C, R, L)
    )
    lon_n, lat_n_blocks = 128, 4

    def packed(cols, rows):
        part = lax.optimization_barrier(ft[cols, :, rows]).astype(jnp.bfloat16)
        return jnp.concatenate([part, masks[0][cols, None, rows].astype(jnp.bfloat16)], axis=1)

    lon_w = lax.ppermute(
        packed(slice(C - 2, C), slice(0, R)), LON, [(i, (i + 1) % lon_n) for i in range(lon_n)]
    )
    lon_e = lax.ppermute(
        packed(slice(0, 2), slice(0, R)), LON, [((i + 1) % lon_n, i) for i in range(lon_n)]
    )

    def wide(rows):
        return jnp.concatenate(
            [lon_w[1:, :, rows], packed(slice(0, C), rows), lon_e[:1, :, rows]], axis=0
        )

    ends = range(lat_n_blocks - 1)
    lat_s = lax.ppermute(wide(slice(R - 2, R)), LAT, [(i, i + 1) for i in ends])
    lat_n = lax.ppermute(wide(slice(0, 2)), LAT, [(i + 1, i) for i in ends])

    prepare = pl.pallas_call(
        prepare_kernel,
        out_shape=(
            jax.ShapeDtypeStruct((ROWS, IN), jnp.float32),
            jax.ShapeDtypeStruct((ROWS, IN), jnp.bfloat16),
            jax.ShapeDtypeStruct((ROWS, L), jnp.float32),
        ),
        in_specs=vmem(6),
        out_specs=vmem(3),
        scratch_shapes=[
            pltpu.VMEM((C + 4, F, 32, L), jnp.float32),
            pltpu.VMEM((WIDE, F, 8, L), jnp.float32),
        ],
        compiler_params=pltpu.CompilerParams(vmem_limit_bytes=10 << 20),
        name="prepare",
    )
    moved1, x1, mask0 = prepare(ft, masks[0], lon_w, lon_e, lat_s, lat_n)

    result = pl.pallas_call(
        step_kernel,
        out_shape=jax.ShapeDtypeStruct((C, F, R, L), jnp.float32),
        in_specs=[pl.BlockSpec(memory_space=pltpu.SMEM)]
        + vmem(4)
        + [pl.BlockSpec(memory_space=pl.ANY)] * 8,
        out_specs=pl.BlockSpec(memory_space=pltpu.VMEM),
        scratch_shapes=[
            pltpu.VMEM((2, HID, 2 * HALF), jnp.bfloat16),
            pltpu.VMEM((ROWS, HID), jnp.bfloat16),
            pltpu.VMEM((ROWS, HID), jnp.bfloat16),
            pltpu.VMEM((ROWS, IN), jnp.float32),
            pltpu.VMEM((WIDE, F, 32, L), jnp.float32),
            pltpu.VMEM((C * R, IN), jnp.bfloat16),
            pltpu.VMEM((C * R, IN), jnp.float32),
            pltpu.SemaphoreType.DMA((64,)),
        ],
        compiler_params=pltpu.CompilerParams(vmem_limit_bytes=26 << 20),
        name="steps",
    )(table, x1, moved1, mask0, masks[1].reshape(C * R, L), *pieces)
    return result.transpose(2, 0, 1, 3)


def solution(mesh):
    grid = Mesh(mesh.devices.reshape(4, 2, 16, 2, 2), AXES)
    in_specs = (
        P(LAT, LON, None, None),
        P(None, LAT, LON),
        P(None, LON, None),
        P(None, LON, None),
        P(None, LON, None),
    )

    return jax.shard_map(
        shards, mesh=grid, in_specs=in_specs, out_specs=P(LAT, LON, None, None), check_vma=False
    )
```

```python
import jax
import jax.numpy as jnp
import numpy as np
from jax import lax
from jax.experimental import pallas as pl
from jax.experimental.pallas import tpu as pltpu
from jax.sharding import Mesh
from jax.sharding import PartitionSpec as P

COURANT = 0.25
DIFFUSE = 0.1
EPSILON = 1e-06
AXES = ("y", "xl", "z", "xh", "core")
LON = ("y", "xl", "z")
LAT = ("xh", "core")
F, L = 6, 128
C, R = 20, 16
WIDE = C + 2
MAIN = WIDE * R
ROWS = MAIN + 2 * C + 8
IN = F * L
HID = 1024
HALF = 1280
TILE = 256


def ring_partner(i, kind):
    if kind == 0:
        return i ^ 1
    return (i + 1) % 4 if i % 2 else (i - 1) % 4


def x_exchange(a, rnd):
    pairs = []
    for x in range(4):
        for c in range(2):
            p = ring_partner(x, c if rnd == 0 else 1 - c)
            pairs.append(((x % 2) * 4 + (x // 2) * 2 + c, (p % 2) * 4 + (p // 2) * 2 + c))
    return lax.ppermute(a, ("xl", "xh", "core"), pairs)


def y_exchange(a, rnd):
    pairs = []
    for y in range(4):
        for c in range(2):
            p = ring_partner(y, c if rnd == 0 else 1 - c)
            pairs.append((y * 2 + c, p * 2 + c))
    return lax.ppermute(a, ("y", "core"), pairs)


def core_swap(a):
    return lax.ppermute(a, "core", [(0, 1), (1, 0)])


def gather_weights(block):
    z = lax.all_gather(block, "z", axis=0)
    a, b = z[:8], z[8:]
    a1, b1 = x_exchange(a, 0), y_exchange(b, 0)
    a2, b2 = jnp.stack([a, a1]), jnp.stack([b, b1])
    a3, b3 = x_exchange(a2, 1), y_exchange(b2, 1)
    a4, b4 = jnp.concatenate([a2, a3]), jnp.concatenate([b2, b3])
    a5, b5 = y_exchange(a4, 0), x_exchange(b4, 0)
    a6, b6 = jnp.stack([a4, a5]), jnp.stack([b4, b5])
    a7, b7 = y_exchange(a6, 1), x_exchange(b6, 1)
    ca6, cb6 = core_swap(a6), core_swap(b6)
    ca7, cb7 = core_swap(a7), core_swap(b7)
    return [p.reshape(8 * 64, HALF) for p in (a6, a7, b6, b7, ca6, ca7, cb6, cb7)]


def moved_of(cen, east, west, u, v):
    north = pltpu.roll(cen, cen.shape[0] - 1, 0)
    south = pltpu.roll(cen, 1, 0)
    advected = u * (east - west) + v * (north - south)
    smoothed = east + west + north + south - 4.0 * cen
    return cen - COURANT * advected + DIFFUSE * smoothed


def column_moved(ext, c):
    cen = [ext[c, f] for f in range(F)]
    return [moved_of(cen[f], ext[c + 1, f], ext[c - 1, f], cen[0], cen[1]) for f in range(F)]


def rs_of(parts):
    ss = parts[0] * parts[0]
    for p in parts[1:]:
        ss = ss + p * p
    return lax.rsqrt(jnp.sum(ss, axis=-1, keepdims=True) * (1.0 / IN) + EPSILON)


def lanes(f):
    return slice(f * L, (f + 1) * L)


def prepare_kernel(ft, mask, lon_w, lon_e, lat_s, lat_n, moved, normed, mk, ext, edge):
    moved[MAIN:, :] = jnp.zeros((ROWS - MAIN, IN), jnp.float32)
    mk[MAIN:, :] = jnp.zeros((ROWS - MAIN, L), jnp.float32)

    def own(c, carry):
        for f in range(F):
            ext[c + 2, f, 8 : 8 + R, :] = ft[c, f]
        row = pl.multiple_of((c + 1) * R, R)
        mk[pl.ds(row, R), :] = mask[c]
        return carry

    lax.fori_loop(0, C, own, 0)
    for c in range(2):
        for f in range(F):
            ext[c, f, 8 : 8 + R, :] = lon_w[c, f].astype(jnp.float32)
            ext[C + 2 + c, f, 8 : 8 + R, :] = lon_e[c, f].astype(jnp.float32)
    mk[0:R, :] = lon_w[1, F].astype(jnp.float32)
    mk[MAIN - R : MAIN, :] = lon_e[0, F].astype(jnp.float32)

    def sides(c, carry):
        for f in range(F):
            ext[c + 1, f, 6:8, :] = lat_s[c, f].astype(jnp.float32)
            ext[c + 1, f, 8 + R : 10 + R, :] = lat_n[c, f].astype(jnp.float32)
        return carry

    lax.fori_loop(0, WIDE, sides, 0)

    def step(c, carry):
        parts = column_moved(ext, c + 1)
        rs = rs_of(parts)
        row = pl.multiple_of(c * R, R)
        for f in range(F):
            moved[pl.ds(row, R), lanes(f)] = parts[f][8 : 8 + R]
            normed[pl.ds(row, R), lanes(f)] = (parts[f] * rs)[8 : 8 + R].astype(jnp.bfloat16)

        for f in range(F):
            edge[c, f, 0:1, :] = parts[f][7:8]
            edge[c, f, 1:2, :] = parts[f][8 + R : 9 + R]
        return carry

    lax.fori_loop(0, WIDE, step, 0)
    for c in range(C):
        for k, side in enumerate((lat_s, lat_n)):
            row = MAIN + k * C + c
            for f in range(F):
                moved[row : row + 1, lanes(f)] = edge[c + 1, f, k : k + 1, :]
            mk[row : row + 1, :] = side[c + 1, F].astype(jnp.float32)[1 - k : 2 - k]
    tail = [moved[MAIN:, lanes(f)] for f in range(F)]
    rs = rs_of(tail)
    for f in range(F):
        normed[MAIN:, lanes(f)] = (tail[f] * rs).astype(jnp.bfloat16)


def silu(t):
    half = 0.5 * t
    return (half + half * jnp.tanh(half)).astype(jnp.bfloat16)


def networks(x, mask_ref, weights, h1, h2, out, rows, arrive):
    def net(n, carry):
        if arrive:
            arrive(n, 0)
        want = (1 - n).astype(jnp.float32)
        for t in range(HID // TILE):
            w = weights[n, t * TILE : (t + 1) * TILE, 0:IN]
            d = lax.dot_general(x[...], w, (((1,), (1,)), ((), ())), preferred_element_type=jnp.float32)
            h1[0:rows, t * TILE : (t + 1) * TILE] = silu(d)
        if arrive:
            arrive(n, 1)
        for t in range(HID // TILE):
            w = weights[n, :, IN + t * TILE : IN + (t + 1) * TILE]
            d = jnp.dot(h1[0:rows, :], w, preferred_element_type=jnp.float32)
            h2[0:rows, t * TILE : (t + 1) * TILE] = silu(d)
        pick = mask_ref[...].reshape(rows, L) == want
        pick = jnp.concatenate([pick, pick], axis=1)
        for t in range(IN // TILE):
            cols = slice(t * TILE, (t + 1) * TILE)
            w = weights[n, :, IN + HID + t * TILE : IN + HID + (t + 1) * TILE]
            d = jnp.dot(h2[0:rows, :], w, preferred_element_type=jnp.float32)
            out[0:rows, cols] = jnp.where(pick, d, out[0:rows, cols])
        return carry

    lax.fori_loop(0, 2, net, 0)


def step_kernel(positions, x1, moved1_any, mask0, mask1, *rest):
    pieces = rest[:8]
    result = rest[8]
    weights, h1, h2, out, ext, x2, moved2, moved1, sems, moved_sem = rest[9:]
    at = lax.axis_index("y") * 8 + lax.axis_index("xl") * 4 + lax.axis_index("xh") * 2 + lax.axis_index("core")
    base = at * 32

    def table(k):
        return positions[base + k]

    core = table(16)
    for k in range(8):
        net = core if k < 4 else 1 - core
        colour = (k // 2) % 2
        late = (k % 2) * 2
        for p in range(2):
            for q in range(4):
                j, i = (late + p, q) if colour == 0 else (q, late + p)
                x = table(net * 8 + i)
                y = table(net * 8 + 4 + j)
                row = pl.multiple_of(y * 256 + (x % 2) * 128 + colour * 64, 64)
                col = pl.multiple_of((x // 2) * HALF, 128)
                src = pieces[k].at[pl.ds((p * 4 + q) * 64, 64), :]
                dst = weights.at[net, pl.ds(row, 64), pl.ds(col, HALF)]
                sem = (net * 2 + x // 2) * 16 + y * 4 + (x % 2) * 2 + colour
                pltpu.make_async_copy(src, dst, sems.at[sem]).start()

    arrived = pltpu.make_async_copy(moved1_any, moved1, moved_sem)
    arrived.start()

    def arrive(net, half):
        for k in range(16):
            src = pieces[0].at[pl.ds(0, 64), :]
            dst = weights.at[net, pl.ds(k * 64, 64), pl.ds(half * HALF, HALF)]
            pltpu.make_async_copy(src, dst, sems.at[(net * 2 + half) * 16 + k]).wait()

    networks(x1, mask0, weights, h1, h2, out, ROWS, arrive)
    arrived.wait()

    def spread(c, carry):
        row = pl.multiple_of(c * R, R)
        for f in range(F):
            ext[c, f, 8 : 8 + R, :] = moved1[pl.ds(row, R), lanes(f)] + out[pl.ds(row, R), lanes(f)]
        return carry

    lax.fori_loop(0, WIDE, spread, 0)

    for c in range(C):
        for k, (at, flag) in enumerate(((7, 17), (8 + R, 18))):
            row = MAIN + k * C + c
            value = moved1[row : row + 1, :] + out[row : row + 1, :]
            value = jnp.where(table(flag) == 1, value, jnp.zeros_like(value))
            for f in range(F):
                ext[c + 1, f, at : at + 1, :] = value[:, lanes(f)]

    def second(c, carry):
        parts = column_moved(ext, c + 1)
        rs = rs_of(parts)
        row = pl.multiple_of(c * R, R)
        for f in range(F):
            moved2[pl.ds(row, R), lanes(f)] = parts[f][8 : 8 + R]
            x2[pl.ds(row, R), lanes(f)] = (parts[f] * rs)[8 : 8 + R].astype(jnp.bfloat16)
        return carry

    lax.fori_loop(0, C, second, 0)
    networks(x2, mask1, weights, h1, h2, out, C * R, None)

    def finish(c, carry):
        row = pl.multiple_of(c * R, R)
        for f in range(F):
            result[c, f] = moved2[pl.ds(row, R), lanes(f)] + out[pl.ds(row, R), lanes(f)]
        return carry

    lax.fori_loop(0, C, finish, 0)


def position_table():
    out = np.zeros((32, 32), np.int32)

    def order(i, net):
        p = ring_partner(i, net)
        n = ring_partner(i, 1 - net)
        return [i, p, n, ring_partner(n, net)]

    for y, xl, xh, core in np.ndindex(4, 2, 2, 2):
        x, lat = xh * 2 + xl, xh * 2 + core
        row = order(x, 0) + order(y, 0) + order(x, 1) + order(y, 1) + [core, int(lat > 0), int(lat < 3)]
        out[((y * 2 + xl) * 2 + xh) * 2 + core, : len(row)] = row
    return out


def vmem(n):
    return [pl.BlockSpec(memory_space=pltpu.VMEM)] * n


def shards(fields, day_mask, w_in, w_mid, w_out):
    xh, core = lax.axis_index("xh"), lax.axis_index("core")
    joined = jnp.concatenate([w_in, w_mid, w_out], axis=2)
    block = lax.dynamic_slice(joined, (core, 0, xh * HALF), (1, 8, HALF))[0]
    pieces = gather_weights(block)

    ft = fields.transpose(1, 2, 0, 3)
    masks = jnp.broadcast_to(
        day_mask.transpose(0, 2, 1)[..., None].astype(jnp.float32), (2, C, R, L)
    )
    lon_n, lat_n_blocks = 128, 4

    def packed(cols, rows):
        part = lax.optimization_barrier(ft[cols, :, rows]).astype(jnp.bfloat16)
        return jnp.concatenate([part, masks[0][cols, None, rows].astype(jnp.bfloat16)], axis=1)

    lon_w = lax.ppermute(
        packed(slice(C - 2, C), slice(0, R)), LON, [(i, (i + 1) % lon_n) for i in range(lon_n)]
    )
    lon_e = lax.ppermute(
        packed(slice(0, 2), slice(0, R)), LON, [((i + 1) % lon_n, i) for i in range(lon_n)]
    )

    def wide(rows):
        return jnp.concatenate(
            [lon_w[1:, :, rows], packed(slice(0, C), rows), lon_e[:1, :, rows]], axis=0
        )

    ends = range(lat_n_blocks - 1)
    lat_s = lax.ppermute(wide(slice(R - 2, R)), LAT, [(i, i + 1) for i in ends])
    lat_n = lax.ppermute(wide(slice(0, 2)), LAT, [(i + 1, i) for i in ends])

    prepare = pl.pallas_call(
        prepare_kernel,
        out_shape=(
            jax.ShapeDtypeStruct((ROWS, IN), jnp.float32),
            jax.ShapeDtypeStruct((ROWS, IN), jnp.bfloat16),
            jax.ShapeDtypeStruct((ROWS, L), jnp.float32),
        ),
        in_specs=vmem(6),
        out_specs=vmem(3),
        scratch_shapes=[
            pltpu.VMEM((C + 4, F, 32, L), jnp.float32),
            pltpu.VMEM((WIDE, F, 8, L), jnp.float32),
        ],
        compiler_params=pltpu.CompilerParams(vmem_limit_bytes=4 << 20),
        name="prepare",
    )
    moved1, x1, mask0 = prepare(ft, masks[0], lon_w, lon_e, lat_s, lat_n)

    result = pl.pallas_call(
        step_kernel,
        out_shape=jax.ShapeDtypeStruct((C, F, R, L), jnp.float32),
        in_specs=[pl.BlockSpec(memory_space=pltpu.SMEM)]
        + vmem(1)
        + [pl.BlockSpec(memory_space=pl.ANY)]
        + vmem(2)
        + [pl.BlockSpec(memory_space=pl.ANY)] * 8,
        out_specs=pl.BlockSpec(memory_space=pltpu.VMEM),
        scratch_shapes=[
            pltpu.VMEM((2, HID, 2 * HALF), jnp.bfloat16),
            pltpu.VMEM((ROWS, HID), jnp.bfloat16),
            pltpu.VMEM((ROWS, HID), jnp.bfloat16),
            pltpu.VMEM((ROWS, IN), jnp.float32),
            pltpu.VMEM((WIDE, F, 32, L), jnp.float32),
            pltpu.VMEM((C * R, IN), jnp.bfloat16),
            pltpu.VMEM((C * R, IN), jnp.float32),
            pltpu.VMEM((ROWS, IN), jnp.float32),
            pltpu.SemaphoreType.DMA((64,)),
            pltpu.SemaphoreType.DMA,
        ],
        compiler_params=pltpu.CompilerParams(vmem_limit_bytes=26 << 20),
        name="steps",
    )(position_table().reshape(-1), x1, moved1, mask0, masks[1], *pieces)
    return result.transpose(2, 0, 1, 3)


def solution(mesh):
    grid = Mesh(mesh.devices.reshape(4, 2, 16, 2, 2), AXES)
    in_specs = (
        P(LAT, LON, None, None),
        P(None, LAT, LON),
        P(None, LON, None),
        P(None, LON, None),
        P(None, LON, None),
    )

    return jax.shard_map(
        shards, mesh=grid, in_specs=in_specs, out_specs=P(LAT, LON, None, None), check_vma=False
    )
```

```python
import jax
import jax.numpy as jnp
import numpy as np
from jax import lax
from jax.experimental import pallas as pl
from jax.experimental.pallas import tpu as pltpu
from jax.sharding import Mesh
from jax.sharding import PartitionSpec as P

COURANT = 0.25
DIFFUSE = 0.1
EPSILON = 1e-06
AXES = ("y", "xl", "z", "xh", "core")
LON = ("y", "xl", "z")
LAT = ("xh", "core")
F, L = 6, 128
C, R = 20, 16
WIDE = C + 2
MAIN = WIDE * R
ROWS = MAIN + 2 * C + 8
IN = F * L
HID = 1024
HALF = 1280
TILE = 256
BLOCK = 128


def ring_partner(i, kind):
    if kind == 0:
        return i ^ 1
    return (i + 1) % 4 if i % 2 else (i - 1) % 4


def exchange(a, kind, first):
    pairs = []
    for y, xl, xh, core in np.ndindex(4, 2, 2, 2):
        x = xh * 2 + xl
        if (core == 0) == (first == "x"):
            px, py = ring_partner(x, kind), y
        else:
            px, py = x, ring_partner(y, kind)
        pairs.append((device_at(y, x, core), device_at(py, px, core)))
    return lax.ppermute(a, ("y", "xl", "xh", "core"), pairs)


def device_at(y, x, core):
    return ((y * 2 + x % 2) * 2 + x // 2) * 2 + core


def core_swap(a):
    return lax.ppermute(a, "core", [(0, 1), (1, 0)])


def gather_weights(block):
    z = lax.all_gather(block, "z", axis=0)
    z1 = exchange(z, 0, "x")
    a = jnp.stack([z, z1])
    b = exchange(a, 1, "x")
    a5, b5 = exchange(a, 0, "y"), exchange(b, 1, "y")
    a6, b6 = jnp.stack([a, a5]), jnp.stack([b, b5])
    a7, b7 = exchange(a6, 1, "y"), exchange(b6, 0, "y")
    ca6, cb6 = core_swap(a6), core_swap(b6)
    ca7, cb7 = core_swap(a7), core_swap(b7)
    return [p.reshape(4 * BLOCK, HALF) for p in (a6, a7, b6, b7, ca6, ca7, cb6, cb7)]


def moved_of(cen, east, west, u, v):
    north = pltpu.roll(cen, cen.shape[0] - 1, 0)
    south = pltpu.roll(cen, 1, 0)
    advected = u * (east - west) + v * (north - south)
    smoothed = east + west + north + south - 4.0 * cen
    return cen - COURANT * advected + DIFFUSE * smoothed


def column_moved(ext, c):
    cen = [ext[c, f] for f in range(F)]
    return [moved_of(cen[f], ext[c + 1, f], ext[c - 1, f], cen[0], cen[1]) for f in range(F)]


def rs_of(parts):
    ss = parts[0] * parts[0]
    for p in parts[1:]:
        ss = ss + p * p
    return lax.rsqrt(jnp.sum(ss, axis=-1, keepdims=True) * (1.0 / IN) + EPSILON)


def lanes(f):
    return slice(f * L, (f + 1) * L)


def mask_kernel(days, first, second):
    for out, step in ((first, 0), (second, 1)):
        m = days[step].astype(jnp.float32)
        for c in range(C):
            out[c] = jnp.broadcast_to(m[:, c : c + 1], (R, L))


def prepare_kernel(ft, mask, lon_w, lon_e, lat_s, lat_n, moved, normed, mk, ext, edge):
    moved[MAIN:, :] = jnp.zeros((ROWS - MAIN, IN), jnp.float32)
    mk[MAIN:, :] = jnp.zeros((ROWS - MAIN, L), jnp.float32)

    def own(c, carry):
        for f in range(F):
            ext[c + 2, f, 8 : 8 + R, :] = ft[c, f]
        row = pl.multiple_of((c + 1) * R, R)
        mk[pl.ds(row, R), :] = mask[c]
        return carry

    lax.fori_loop(0, C, own, 0)
    for c in range(2):
        for f in range(F):
            ext[c, f, 8 : 8 + R, :] = lon_w[c, f].astype(jnp.float32)
            ext[C + 2 + c, f, 8 : 8 + R, :] = lon_e[c, f].astype(jnp.float32)
    mk[0:R, :] = lon_w[1, F].astype(jnp.float32)
    mk[MAIN - R : MAIN, :] = lon_e[0, F].astype(jnp.float32)

    def sides(c, carry):
        for f in range(F):
            ext[c + 1, f, 6:8, :] = lat_s[c, f].astype(jnp.float32)
            ext[c + 1, f, 8 + R : 10 + R, :] = lat_n[c, f].astype(jnp.float32)
        return carry

    lax.fori_loop(0, WIDE, sides, 0)

    def step(c, carry):
        parts = column_moved(ext, c + 1)
        rs = rs_of(parts)
        row = pl.multiple_of(c * R, R)
        for f in range(F):
            moved[pl.ds(row, R), lanes(f)] = parts[f][8 : 8 + R]
            normed[pl.ds(row, R), lanes(f)] = (parts[f] * rs)[8 : 8 + R].astype(jnp.bfloat16)

        for f in range(F):
            edge[c, f, 0:1, :] = parts[f][7:8]
            edge[c, f, 1:2, :] = parts[f][8 + R : 9 + R]
        return carry

    lax.fori_loop(0, WIDE, step, 0)
    for c in range(C):
        for k, side in enumerate((lat_s, lat_n)):
            row = MAIN + k * C + c
            for f in range(F):
                moved[row : row + 1, lanes(f)] = edge[c + 1, f, k : k + 1, :]
            mk[row : row + 1, :] = side[c + 1, F].astype(jnp.float32)[1 - k : 2 - k]
    tail = [moved[MAIN:, lanes(f)] for f in range(F)]
    rs = rs_of(tail)
    for f in range(F):
        normed[MAIN:, lanes(f)] = (tail[f] * rs).astype(jnp.bfloat16)


def silu(t):
    half = 0.5 * t
    return (half + half * jnp.tanh(half)).astype(jnp.bfloat16)


def networks(x, mask_ref, weights, h1, h2, out, rows, arrive):
    def net(n, carry):
        if arrive:
            arrive(n, 0)
        want = (1 - n).astype(jnp.float32)
        for t in range(HID // TILE):
            w = weights[n, t * TILE : (t + 1) * TILE, 0:IN]
            d = lax.dot_general(x[...], w, (((1,), (1,)), ((), ())), preferred_element_type=jnp.float32)
            h1[0:rows, t * TILE : (t + 1) * TILE] = silu(d)
        if arrive:
            arrive(n, 1)
        for t in range(HID // TILE):
            w = weights[n, :, IN + t * TILE : IN + (t + 1) * TILE]
            d = jnp.dot(h1[0:rows, :], w, preferred_element_type=jnp.float32)
            h2[0:rows, t * TILE : (t + 1) * TILE] = silu(d)
        pick = mask_ref[...].reshape(rows, L) == want
        pick = jnp.concatenate([pick, pick], axis=1)
        for t in range(IN // TILE):
            cols = slice(t * TILE, (t + 1) * TILE)
            w = weights[n, :, IN + HID + t * TILE : IN + HID + (t + 1) * TILE]
            d = jnp.dot(h2[0:rows, :], w, preferred_element_type=jnp.float32)
            out[0:rows, cols] = jnp.where(pick, d, out[0:rows, cols])
        return carry

    lax.fori_loop(0, 2, net, 0)


def step_kernel(positions, x1, moved1_any, mask0, mask1, *rest):
    pieces = rest[:8]
    result = rest[8]
    weights, h1, h2, out, ext, x2, moved2, moved1, sems, moved_sem = rest[9:]
    at = lax.axis_index("y") * 8 + lax.axis_index("xl") * 4 + lax.axis_index("xh") * 2 + lax.axis_index("core")
    base = at * 32
    lat = lax.axis_index("xh") * 2 + lax.axis_index("core")
    for k in range(8):
        for slot in range(4):
            code = positions[base + k * 4 + slot]
            row = pl.multiple_of((code % 8) * BLOCK, BLOCK)
            col = pl.multiple_of(((code // 8) % 2) * HALF, 128)
            src = pieces[k].at[pl.ds(slot * BLOCK, BLOCK), :]
            dst = weights.at[code // 16, pl.ds(row, BLOCK), pl.ds(col, HALF)]
            pltpu.make_async_copy(src, dst, sems.at[code]).start()

    arrived = pltpu.make_async_copy(moved1_any, moved1, moved_sem)
    arrived.start()

    def arrive(net, half):
        for k in range(8):
            src = pieces[0].at[pl.ds(0, BLOCK), :]
            dst = weights.at[net, pl.ds(k * BLOCK, BLOCK), pl.ds(half * HALF, HALF)]
            pltpu.make_async_copy(src, dst, sems.at[(net * 2 + half) * 8 + k]).wait()

    networks(x1, mask0, weights, h1, h2, out, ROWS, arrive)
    arrived.wait()

    def spread(c, carry):
        row = pl.multiple_of(c * R, R)
        for f in range(F):
            ext[c, f, 8 : 8 + R, :] = moved1[pl.ds(row, R), lanes(f)] + out[pl.ds(row, R), lanes(f)]
        return carry

    lax.fori_loop(0, WIDE, spread, 0)

    for c in range(C):
        for k, (at, exists) in enumerate(((7, lat > 0), (8 + R, lat < 3))):
            row = MAIN + k * C + c
            value = moved1[row : row + 1, :] + out[row : row + 1, :]
            value = jnp.where(exists, value, jnp.zeros_like(value))
            for f in range(F):
                ext[c + 1, f, at : at + 1, :] = value[:, lanes(f)]

    def second(c, carry):
        parts = column_moved(ext, c + 1)
        rs = rs_of(parts)
        row = pl.multiple_of(c * R, R)
        for f in range(F):
            moved2[pl.ds(row, R), lanes(f)] = parts[f][8 : 8 + R]
            x2[pl.ds(row, R), lanes(f)] = (parts[f] * rs)[8 : 8 + R].astype(jnp.bfloat16)
        return carry

    lax.fori_loop(0, C, second, 0)
    networks(x2, mask1, weights, h1, h2, out, C * R, None)

    def finish(c, carry):
        row = pl.multiple_of(c * R, R)
        for f in range(F):
            result[c, f] = moved2[pl.ds(row, R), lanes(f)] + out[pl.ds(row, R), lanes(f)]
        return carry

    lax.fori_loop(0, C, finish, 0)


def position_table():
    out = np.zeros((32, 32), np.int32)

    def order(i, kind):
        n = ring_partner(i, 1 - kind)
        return [i, ring_partner(i, kind), n, ring_partner(n, kind)]

    for y, x, core in np.ndindex(4, 4, 2):
        codes = []
        for k, p, q in np.ndindex(8, 2, 2):
            net = core if k < 4 else 1 - core
            half, late = (k // 2) % 2, (k % 2) * 2
            if net == 0:
                bx, by = order(x, 0)[2 * half + q], order(y, half)[late + p]
            else:
                bx, by = order(x, half)[late + p], order(y, 0)[2 * half + q]
            codes.append((net * 2 + bx // 2) * 8 + by * 2 + bx % 2)
        out[device_at(y, x, core)] = codes
    return out


def vmem(n):
    return [pl.BlockSpec(memory_space=pltpu.VMEM)] * n


def shards(fields, day_mask, w_in, w_mid, w_out):
    xh, core = lax.axis_index("xh"), lax.axis_index("core")
    joined = jnp.concatenate([w_in, w_mid, w_out], axis=2)
    block = lax.dynamic_slice(joined, (core, 0, xh * HALF), (1, 8, HALF))[0]
    pieces = gather_weights(block)

    ft = fields.transpose(1, 2, 0, 3)
    spread_masks = pl.pallas_call(
        mask_kernel,
        out_shape=(jax.ShapeDtypeStruct((C, R, L), jnp.float32),) * 2,
        in_specs=vmem(1),
        out_specs=vmem(2),
        compiler_params=pltpu.CompilerParams(vmem_limit_bytes=4 << 20),
        name="masks",
    )
    masks = spread_masks(day_mask)
    lon_n, lat_n_blocks = 128, 4

    def packed(cols, rows):
        part = lax.optimization_barrier(ft[cols, :, rows]).astype(jnp.bfloat16)
        return jnp.concatenate([part, masks[0][cols, None, rows].astype(jnp.bfloat16)], axis=1)

    lon_w = lax.ppermute(
        packed(slice(C - 2, C), slice(0, R)), LON, [(i, (i + 1) % lon_n) for i in range(lon_n)]
    )
    lon_e = lax.ppermute(
        packed(slice(0, 2), slice(0, R)), LON, [((i + 1) % lon_n, i) for i in range(lon_n)]
    )

    def wide(rows):
        return jnp.concatenate(
            [lon_w[1:, :, rows], packed(slice(0, C), rows), lon_e[:1, :, rows]], axis=0
        )

    ends = range(lat_n_blocks - 1)
    lat_s = lax.ppermute(wide(slice(R - 2, R)), LAT, [(i, i + 1) for i in ends])
    lat_n = lax.ppermute(wide(slice(0, 2)), LAT, [(i + 1, i) for i in ends])

    prepare = pl.pallas_call(
        prepare_kernel,
        out_shape=(
            jax.ShapeDtypeStruct((ROWS, IN), jnp.float32),
            jax.ShapeDtypeStruct((ROWS, IN), jnp.bfloat16),
            jax.ShapeDtypeStruct((ROWS, L), jnp.float32),
        ),
        in_specs=vmem(6),
        out_specs=vmem(3),
        scratch_shapes=[
            pltpu.VMEM((C + 4, F, 32, L), jnp.float32),
            pltpu.VMEM((WIDE, F, 8, L), jnp.float32),
        ],
        compiler_params=pltpu.CompilerParams(vmem_limit_bytes=4 << 20),
        name="prepare",
    )
    moved1, x1, mask0 = prepare(ft, masks[0], lon_w, lon_e, lat_s, lat_n)

    result = pl.pallas_call(
        step_kernel,
        out_shape=jax.ShapeDtypeStruct((C, F, R, L), jnp.float32),
        in_specs=[pl.BlockSpec(memory_space=pltpu.SMEM)]
        + vmem(1)
        + [pl.BlockSpec(memory_space=pl.ANY)]
        + vmem(2)
        + [pl.BlockSpec(memory_space=pl.ANY)] * 8,
        out_specs=pl.BlockSpec(memory_space=pltpu.VMEM),
        scratch_shapes=[
            pltpu.VMEM((2, HID, 2 * HALF), jnp.bfloat16),
            pltpu.VMEM((ROWS, HID), jnp.bfloat16),
            pltpu.VMEM((ROWS, HID), jnp.bfloat16),
            pltpu.VMEM((ROWS, IN), jnp.float32),
            pltpu.VMEM((WIDE, F, 32, L), jnp.float32),
            pltpu.VMEM((C * R, IN), jnp.bfloat16),
            pltpu.VMEM((C * R, IN), jnp.float32),
            pltpu.VMEM((ROWS, IN), jnp.float32),
            pltpu.SemaphoreType.DMA((32,)),
            pltpu.SemaphoreType.DMA,
        ],
        compiler_params=pltpu.CompilerParams(vmem_limit_bytes=26 << 20),
        name="steps",
    )(position_table().reshape(-1), x1, moved1, mask0, masks[1], *pieces)
    return result.transpose(2, 0, 1, 3)


def solution(mesh):
    grid = Mesh(mesh.devices.reshape(4, 2, 16, 2, 2), AXES)
    in_specs = (
        P(LAT, LON, None, None),
        P(None, LAT, LON),
        P(None, LON, None),
        P(None, LON, None),
        P(None, LON, None),
    )

    return jax.shard_map(
        shards, mesh=grid, in_specs=in_specs, out_specs=P(LAT, LON, None, None), check_vma=False
    )
```

```python
import jax
import jax.numpy as jnp
import numpy as np
from jax import lax
from jax.experimental import pallas as pl
from jax.experimental.pallas import tpu as pltpu
from jax.sharding import Mesh
from jax.sharding import PartitionSpec as P

COURANT = 0.25
DIFFUSE = 0.1
EPSILON = 1e-06
AXES = ("y", "xl", "z", "xh", "core")
LON = ("y", "xl", "z")
LAT = ("xh", "core")
F, L = 6, 128
C, R = 20, 16
WIDE = C + 2
MAIN = WIDE * R
ROWS = MAIN + 2 * C + 8
IN = F * L
HID = 1024
HALF = 1280
TILE = 256
BLOCK = 128


def ring_partner(i, kind):
    if kind == 0:
        return i ^ 1
    return (i + 1) % 4 if i % 2 else (i - 1) % 4


def exchange(a, kind, first):
    pairs = []
    for y, xl, xh, core in np.ndindex(4, 2, 2, 2):
        x = xh * 2 + xl
        if (core == 0) == (first == "x"):
            px, py = ring_partner(x, kind), y
        else:
            px, py = x, ring_partner(y, kind)
        pairs.append((device_at(y, x, core), device_at(py, px, core)))
    return lax.ppermute(a, ("y", "xl", "xh", "core"), pairs)


def device_at(y, x, core):
    return ((y * 2 + x % 2) * 2 + x // 2) * 2 + core


def core_swap(a):
    return lax.ppermute(a, "core", [(0, 1), (1, 0)])


def gather_weights(block):
    z = lax.all_gather(block, "z", axis=0)
    z1 = exchange(z, 0, "x")
    a = jnp.stack([z, z1])
    b = exchange(a, 1, "x")
    a5, b5 = exchange(a, 0, "y"), exchange(b, 1, "y")
    a6, b6 = jnp.stack([a, a5]), jnp.stack([b, b5])
    a7, b7 = exchange(a6, 1, "y"), exchange(b6, 0, "y")
    ca6, cb6 = core_swap(a6), core_swap(b6)
    ca7, cb7 = core_swap(a7), core_swap(b7)
    return [p.reshape(4 * BLOCK, HALF) for p in (a6, a7, b6, b7, ca6, ca7, cb6, cb7)]


def moved_of(cen, east, west, u, v):
    north = pltpu.roll(cen, cen.shape[0] - 1, 0)
    south = pltpu.roll(cen, 1, 0)
    advected = u * (east - west) + v * (north - south)
    smoothed = east + west + north + south - 4.0 * cen
    return cen - COURANT * advected + DIFFUSE * smoothed


def column_moved(ext, c):
    cen = [ext[c, f] for f in range(F)]
    return [moved_of(cen[f], ext[c + 1, f], ext[c - 1, f], cen[0], cen[1]) for f in range(F)]


def own_moved(ext, c):
    rows = slice(8, 8 + R)
    cen = [ext[c, f, rows, :] for f in range(F)]
    u, v = COURANT * cen[0], COURANT * cen[1]
    out = []
    for f in range(F):
        east, west = ext[c + 1, f, rows, :], ext[c - 1, f, rows, :]
        north, south = ext[c, f, 9 : 9 + R, :], ext[c, f, 7 : 7 + R, :]
        advected = u * (east - west) + v * (north - south)
        smoothed = (east + west) + (north + south) - 4.0 * cen[f]
        out.append(cen[f] - advected + DIFFUSE * smoothed)
    return out


def rs_of(parts):
    ss = parts[0] * parts[0]
    for p in parts[1:]:
        ss = ss + p * p
    return lax.rsqrt(jnp.sum(ss, axis=-1, keepdims=True) * (1.0 / IN) + EPSILON)


def lanes(f):
    return slice(f * L, (f + 1) * L)


def mask_kernel(days, first, second):
    for out, step in ((first, 0), (second, 1)):
        m = days[step].astype(jnp.float32)
        for c in range(C):
            out[c] = jnp.broadcast_to(m[:, c : c + 1], (R, L))


def prepare_kernel(ft, mask, lon_w, lon_e, lat_s, lat_n, moved, normed, mk, ext, edge):
    moved[MAIN:, :] = jnp.zeros((ROWS - MAIN, IN), jnp.float32)
    mk[MAIN:, :] = jnp.zeros((ROWS - MAIN, L), jnp.float32)

    def own(c, carry):
        for f in range(F):
            ext[c + 2, f, 8 : 8 + R, :] = ft[c, f]
        row = pl.multiple_of((c + 1) * R, R)
        mk[pl.ds(row, R), :] = mask[c]
        return carry

    lax.fori_loop(0, C, own, 0)
    for c in range(2):
        for f in range(F):
            ext[c, f, 8 : 8 + R, :] = lon_w[c, f].astype(jnp.float32)
            ext[C + 2 + c, f, 8 : 8 + R, :] = lon_e[c, f].astype(jnp.float32)
    mk[0:R, :] = lon_w[1, F].astype(jnp.float32)
    mk[MAIN - R : MAIN, :] = lon_e[0, F].astype(jnp.float32)

    def sides(c, carry):
        for f in range(F):
            ext[c + 1, f, 6:8, :] = lat_s[c, f].astype(jnp.float32)
            ext[c + 1, f, 8 + R : 10 + R, :] = lat_n[c, f].astype(jnp.float32)
        return carry

    lax.fori_loop(0, WIDE, sides, 0)

    def step(c, carry):
        parts = column_moved(ext, c + 1)
        rs = rs_of(parts)
        row = pl.multiple_of(c * R, R)
        for f in range(F):
            moved[pl.ds(row, R), lanes(f)] = parts[f][8 : 8 + R]
            normed[pl.ds(row, R), lanes(f)] = (parts[f] * rs)[8 : 8 + R].astype(jnp.bfloat16)

        for f in range(F):
            edge[c, f, 0:1, :] = parts[f][7:8]
            edge[c, f, 1:2, :] = parts[f][8 + R : 9 + R]
        return carry

    lax.fori_loop(0, WIDE, step, 0)
    for c in range(C):
        for k, side in enumerate((lat_s, lat_n)):
            row = MAIN + k * C + c
            for f in range(F):
                moved[row : row + 1, lanes(f)] = edge[c + 1, f, k : k + 1, :]
            mk[row : row + 1, :] = side[c + 1, F].astype(jnp.float32)[1 - k : 2 - k]
    tail = [moved[MAIN:, lanes(f)] for f in range(F)]
    rs = rs_of(tail)
    for f in range(F):
        normed[MAIN:, lanes(f)] = (tail[f] * rs).astype(jnp.bfloat16)


def silu(t):
    half = 0.5 * t
    return (half + half * jnp.tanh(half)).astype(jnp.bfloat16)


def networks(core, x, mask_ref, weights, h1, h2, out, rows, arrive):
    def net(n, initial):
        if arrive:
            arrive(n, 0)
        want = (1 - n).astype(jnp.float32)
        for t in range(HID // TILE):
            w = weights[n, t * TILE : (t + 1) * TILE, 0:IN]
            d = lax.dot_general(x[...], w, (((1,), (1,)), ((), ())), preferred_element_type=jnp.float32)
            h1[0:rows, t * TILE : (t + 1) * TILE] = silu(d)
        if arrive:
            arrive(n, 1)
        for t in range(HID // TILE):
            w = weights[n, :, IN + t * TILE : IN + (t + 1) * TILE]
            d = jnp.dot(h1[0:rows, :], w, preferred_element_type=jnp.float32)
            h2[0:rows, t * TILE : (t + 1) * TILE] = silu(d)
        pick = mask_ref[...].reshape(rows, L) == want
        pick = jnp.concatenate([pick, pick], axis=1)
        for t in range(IN // TILE):
            cols = slice(t * TILE, (t + 1) * TILE)
            w = weights[n, :, IN + HID + t * TILE : IN + HID + (t + 1) * TILE]
            d = jnp.dot(h2[0:rows, :], w, preferred_element_type=jnp.float32)
            out[0:rows, cols] = jnp.where(pick, d, 0.0 if initial else out[0:rows, cols])

    net(core, True)
    net(1 - core, False)


def step_kernel(positions, x1, moved1_any, mask0, mask1, *rest):
    pieces = rest[:8]
    result = rest[8]
    weights, h1, h2, out, ext, x2, moved2, moved1, sems, moved_sem = rest[9:]
    at = lax.axis_index("y") * 8 + lax.axis_index("xl") * 4 + lax.axis_index("xh") * 2 + lax.axis_index("core")
    core = lax.axis_index("core")
    base = at * 32
    lat = lax.axis_index("xh") * 2 + lax.axis_index("core")
    for k in range(8):
        for slot in range(4):
            code = positions[base + k * 4 + slot]
            row = pl.multiple_of((code % 8) * BLOCK, BLOCK)
            col = pl.multiple_of(((code // 8) % 2) * HALF, 128)
            src = pieces[k].at[pl.ds(slot * BLOCK, BLOCK), :]
            dst = weights.at[code // 16, pl.ds(row, BLOCK), pl.ds(col, HALF)]
            pltpu.make_async_copy(src, dst, sems.at[code]).start()

    arrived = pltpu.make_async_copy(moved1_any, moved1, moved_sem)
    arrived.start()

    def arrive(net, half):
        for k in range(8):
            src = pieces[0].at[pl.ds(0, BLOCK), :]
            dst = weights.at[net, pl.ds(k * BLOCK, BLOCK), pl.ds(half * HALF, HALF)]
            pltpu.make_async_copy(src, dst, sems.at[(net * 2 + half) * 8 + k]).wait()

    networks(core, x1, mask0, weights, h1, h2, out, ROWS, arrive)
    arrived.wait()

    def spread(c, carry):
        row = pl.multiple_of(c * R, R)
        for f in range(F):
            ext[c, f, 8 : 8 + R, :] = moved1[pl.ds(row, R), lanes(f)] + out[pl.ds(row, R), lanes(f)]
        return carry

    lax.fori_loop(0, WIDE, spread, 0, unroll=True)

    for c in range(C):
        for k, (at, exists) in enumerate(((7, lat > 0), (8 + R, lat < 3))):
            row = MAIN + k * C + c
            value = moved1[row : row + 1, :] + out[row : row + 1, :]
            value = jnp.where(exists, value, jnp.zeros_like(value))
            for f in range(F):
                ext[c + 1, f, at : at + 1, :] = value[:, lanes(f)]

    def second(c, carry):
        parts = own_moved(ext, c + 1)
        rs = rs_of(parts)
        row = pl.multiple_of(c * R, R)
        for f in range(F):
            moved2[pl.ds(row, R), lanes(f)] = parts[f]
            x2[pl.ds(row, R), lanes(f)] = (parts[f] * rs).astype(jnp.bfloat16)
        return carry

    lax.fori_loop(0, C, second, 0, unroll=5)
    networks(core, x2, mask1, weights, h1, h2, out, C * R, None)

    def finish(c, carry):
        row = pl.multiple_of(c * R, R)
        for f in range(F):
            result[c, f] = moved2[pl.ds(row, R), lanes(f)] + out[pl.ds(row, R), lanes(f)]
        return carry

    lax.fori_loop(0, C, finish, 0, unroll=True)


def position_table():
    out = np.zeros((32, 32), np.int32)

    def order(i, kind):
        n = ring_partner(i, 1 - kind)
        return [i, ring_partner(i, kind), n, ring_partner(n, kind)]

    for y, x, core in np.ndindex(4, 4, 2):
        codes = []
        for k, p, q in np.ndindex(8, 2, 2):
            net = core if k < 4 else 1 - core
            half, late = (k // 2) % 2, (k % 2) * 2
            if net == 0:
                bx, by = order(x, 0)[2 * half + q], order(y, half)[late + p]
            else:
                bx, by = order(x, half)[late + p], order(y, 0)[2 * half + q]
            codes.append((net * 2 + bx // 2) * 8 + by * 2 + bx % 2)
        out[device_at(y, x, core)] = codes
    return out


def vmem(n):
    return [pl.BlockSpec(memory_space=pltpu.VMEM)] * n


def steps_call():
    return pl.pallas_call(
        step_kernel,
        out_shape=jax.ShapeDtypeStruct((C, F, R, L), jnp.float32),
        in_specs=[pl.BlockSpec(memory_space=pltpu.SMEM)]
        + vmem(1)
        + [pl.BlockSpec(memory_space=pl.ANY)]
        + vmem(2)
        + [pl.BlockSpec(memory_space=pl.ANY)] * 8,
        out_specs=pl.BlockSpec(memory_space=pltpu.VMEM),
        scratch_shapes=[
            pltpu.VMEM((2, HID, 2 * HALF), jnp.bfloat16),
            pltpu.VMEM((ROWS, HID), jnp.bfloat16),
            pltpu.VMEM((ROWS, HID), jnp.bfloat16),
            pltpu.VMEM((ROWS, IN), jnp.float32),
            pltpu.VMEM((WIDE, F, 32, L), jnp.float32),
            pltpu.VMEM((C * R, IN), jnp.bfloat16),
            pltpu.VMEM((C * R, IN), jnp.float32),
            pltpu.VMEM((ROWS, IN), jnp.float32),
            pltpu.SemaphoreType.DMA((32,)),
            pltpu.SemaphoreType.DMA,
        ],
        compiler_params=pltpu.CompilerParams(vmem_limit_bytes=26 << 20),
        name="steps",
    )


def shards(fields, day_mask, w_in, w_mid, w_out):
    xh, core = lax.axis_index("xh"), lax.axis_index("core")
    joined = jnp.concatenate([w_in, w_mid, w_out], axis=2)
    block = lax.dynamic_slice(joined, (core, 0, xh * HALF), (1, 8, HALF))[0]
    pieces = gather_weights(block)

    ft = fields.transpose(1, 2, 0, 3)
    spread_masks = pl.pallas_call(
        mask_kernel,
        out_shape=(jax.ShapeDtypeStruct((C, R, L), jnp.float32),) * 2,
        in_specs=vmem(1),
        out_specs=vmem(2),
        compiler_params=pltpu.CompilerParams(vmem_limit_bytes=4 << 20),
        name="masks",
    )
    masks = spread_masks(day_mask)
    lon_n, lat_n_blocks = 128, 4

    def packed(cols, rows):
        part = lax.optimization_barrier(ft[cols, :, rows]).astype(jnp.bfloat16)
        return jnp.concatenate([part, masks[0][cols, None, rows].astype(jnp.bfloat16)], axis=1)

    lon_w = lax.ppermute(
        packed(slice(C - 2, C), slice(0, R)), LON, [(i, (i + 1) % lon_n) for i in range(lon_n)]
    )
    lon_e = lax.ppermute(
        packed(slice(0, 2), slice(0, R)), LON, [((i + 1) % lon_n, i) for i in range(lon_n)]
    )

    def wide(rows):
        return jnp.concatenate(
            [lon_w[1:, :, rows], packed(slice(0, C), rows), lon_e[:1, :, rows]], axis=0
        )

    ends = range(lat_n_blocks - 1)
    lat_s = lax.ppermute(wide(slice(R - 2, R)), LAT, [(i, i + 1) for i in ends])
    lat_n = lax.ppermute(wide(slice(0, 2)), LAT, [(i + 1, i) for i in ends])

    prepare = pl.pallas_call(
        prepare_kernel,
        out_shape=(
            jax.ShapeDtypeStruct((ROWS, IN), jnp.float32),
            jax.ShapeDtypeStruct((ROWS, IN), jnp.bfloat16),
            jax.ShapeDtypeStruct((ROWS, L), jnp.float32),
        ),
        in_specs=vmem(6),
        out_specs=vmem(3),
        scratch_shapes=[
            pltpu.VMEM((C + 4, F, 32, L), jnp.float32),
            pltpu.VMEM((WIDE, F, 8, L), jnp.float32),
        ],
        compiler_params=pltpu.CompilerParams(vmem_limit_bytes=4 << 20),
        name="prepare",
    )
    moved1, x1, mask0 = prepare(ft, masks[0], lon_w, lon_e, lat_s, lat_n)

    result = steps_call()(position_table().reshape(-1), x1, moved1, mask0, masks[1], *pieces)
    return result.transpose(2, 0, 1, 3)


def solution(mesh):
    grid = Mesh(mesh.devices.reshape(4, 2, 16, 2, 2), AXES)
    in_specs = (
        P(LAT, LON, None, None),
        P(None, LAT, LON),
        P(None, LON, None),
        P(None, LON, None),
        P(None, LON, None),
    )

    return jax.shard_map(
        shards, mesh=grid, in_specs=in_specs, out_specs=P(LAT, LON, None, None), check_vma=False
    )
```

```python
import jax
import jax.numpy as jnp
import numpy as np
from jax import lax
from jax.experimental import pallas as pl
from jax.experimental.pallas import tpu as pltpu
from jax.sharding import Mesh
from jax.sharding import PartitionSpec as P

COURANT = 0.25
DIFFUSE = 0.1
EPSILON = 1e-06
AXES = ("y", "xl", "z", "xh", "core")
LON = ("y", "xl", "z")
LAT = ("xh", "core")
F, L = 6, 128
C, R = 20, 16
WIDE = C + 2
MAIN = WIDE * R
ROWS = MAIN + 2 * C + 8
IN = F * L
HID = 1024
HALF = 1280
TILE = 256
BLOCK = 128


def ring_partner(i, kind):
    if kind == 0:
        return i ^ 1
    return (i + 1) % 4 if i % 2 else (i - 1) % 4


def exchange(a, kind, first):
    pairs = []
    for y, xl, xh, core in np.ndindex(4, 2, 2, 2):
        x = xh * 2 + xl
        if (core == 0) == (first == "x"):
            px, py = ring_partner(x, kind), y
        else:
            px, py = x, ring_partner(y, kind)
        pairs.append((device_at(y, x, core), device_at(py, px, core)))
    return lax.ppermute(a, ("y", "xl", "xh", "core"), pairs)


def device_at(y, x, core):
    return ((y * 2 + x % 2) * 2 + x // 2) * 2 + core


def core_swap(a):
    return lax.ppermute(a, "core", [(0, 1), (1, 0)])


def gather_weights(block):
    z = lax.all_gather(block, "z", axis=0)
    z1 = exchange(z, 0, "x")
    a = jnp.stack([z, z1])
    b = exchange(a, 1, "x")
    a5, b5 = exchange(a, 0, "y"), exchange(b, 1, "y")
    a6, b6 = jnp.stack([a, a5]), jnp.stack([b, b5])
    a7, b7 = exchange(a6, 1, "y"), exchange(b6, 0, "y")
    ca6, cb6 = core_swap(a6), core_swap(b6)
    ca7, cb7 = core_swap(a7), core_swap(b7)
    return [p.reshape(4 * BLOCK, HALF) for p in (a6, a7, b6, b7, ca6, ca7, cb6, cb7)]


def moved_of(cen, east, west, u, v):
    north = pltpu.roll(cen, cen.shape[0] - 1, 0)
    south = pltpu.roll(cen, 1, 0)
    advected = u * (east - west) + v * (north - south)
    smoothed = east + west + north + south - 4.0 * cen
    return cen - COURANT * advected + DIFFUSE * smoothed


def column_moved(ext, c):
    cen = [ext[c, f] for f in range(F)]
    return [moved_of(cen[f], ext[c + 1, f], ext[c - 1, f], cen[0], cen[1]) for f in range(F)]


def own_moved(ext, c):
    rows = slice(8, 8 + R)
    cen = [ext[c, f, rows, :] for f in range(F)]
    u, v = COURANT * cen[0], COURANT * cen[1]
    out = []
    for f in range(F):
        east, west = ext[c + 1, f, rows, :], ext[c - 1, f, rows, :]
        north, south = ext[c, f, 9 : 9 + R, :], ext[c, f, 7 : 7 + R, :]
        advected = u * (east - west) + v * (north - south)
        smoothed = (east + west) + (north + south) - 4.0 * cen[f]
        out.append(cen[f] - advected + DIFFUSE * smoothed)
    return out


def rs_of(parts):
    ss = parts[0] * parts[0]
    for p in parts[1:]:
        ss = ss + p * p
    return lax.rsqrt(jnp.sum(ss, axis=-1, keepdims=True) * (1.0 / IN) + EPSILON)


def lanes(f):
    return slice(f * L, (f + 1) * L)


def mask_kernel(days, first, second):
    for out, step in ((first, 0), (second, 1)):
        m = days[step].astype(jnp.float32)
        for c in range(C):
            out[c] = jnp.broadcast_to(m[:, c : c + 1], (R, L))


def prepare_kernel(ft, mask, lon_w, lon_e, lat_s, lat_n, moved, normed, mk, ext, edge):
    moved[MAIN:, :] = jnp.zeros((ROWS - MAIN, IN), jnp.float32)
    mk[MAIN:, :] = jnp.zeros((ROWS - MAIN, L), jnp.float32)

    def own(c, carry):
        for f in range(F):
            ext[c + 2, f, 8 : 8 + R, :] = ft[c, f]
        row = pl.multiple_of((c + 1) * R, R)
        mk[pl.ds(row, R), :] = mask[c]
        return carry

    lax.fori_loop(0, C, own, 0)
    for c in range(2):
        for f in range(F):
            ext[c, f, 8 : 8 + R, :] = lon_w[c, f].astype(jnp.float32)
            ext[C + 2 + c, f, 8 : 8 + R, :] = lon_e[c, f].astype(jnp.float32)
    mk[0:R, :] = lon_w[1, F].astype(jnp.float32)
    mk[MAIN - R : MAIN, :] = lon_e[0, F].astype(jnp.float32)

    def sides(c, carry):
        for f in range(F):
            ext[c + 1, f, 6:8, :] = lat_s[c, f].astype(jnp.float32)
            ext[c + 1, f, 8 + R : 10 + R, :] = lat_n[c, f].astype(jnp.float32)
        return carry

    lax.fori_loop(0, WIDE, sides, 0)

    def step(c, carry):
        parts = column_moved(ext, c + 1)
        rs = rs_of(parts)
        row = pl.multiple_of(c * R, R)
        for f in range(F):
            moved[pl.ds(row, R), lanes(f)] = parts[f][8 : 8 + R]
            normed[pl.ds(row, R), lanes(f)] = (parts[f] * rs)[8 : 8 + R].astype(jnp.bfloat16)

        for f in range(F):
            edge[c, f, 0:1, :] = parts[f][7:8]
            edge[c, f, 1:2, :] = parts[f][8 + R : 9 + R]
        return carry

    lax.fori_loop(0, WIDE, step, 0)
    for c in range(C):
        for k, side in enumerate((lat_s, lat_n)):
            row = MAIN + k * C + c
            for f in range(F):
                moved[row : row + 1, lanes(f)] = edge[c + 1, f, k : k + 1, :]
            mk[row : row + 1, :] = side[c + 1, F].astype(jnp.float32)[1 - k : 2 - k]
    tail = [moved[MAIN:, lanes(f)] for f in range(F)]
    rs = rs_of(tail)
    for f in range(F):
        normed[MAIN:, lanes(f)] = (tail[f] * rs).astype(jnp.bfloat16)


def silu(t):
    half = 0.5 * t
    return (half + half * jnp.tanh(half)).astype(jnp.bfloat16)


def networks(core, x, mask_ref, weights, h1, h2, out, rows, arrive):
    def net(n, initial):
        if arrive:
            arrive(n, 0)
        want = (1 - n).astype(jnp.float32)
        for t in range(HID // TILE):
            w = weights[n, t * TILE : (t + 1) * TILE, 0:IN]
            d = lax.dot_general(x[...], w, (((1,), (1,)), ((), ())), preferred_element_type=jnp.float32)
            h1[0:rows, t * TILE : (t + 1) * TILE] = silu(d)
        if arrive:
            arrive(n, 1)
        for t in range(HID // TILE):
            w = weights[n, :, IN + t * TILE : IN + (t + 1) * TILE]
            d = jnp.dot(h1[0:rows, :], w, preferred_element_type=jnp.float32)
            h2[0:rows, t * TILE : (t + 1) * TILE] = silu(d)
        pick = mask_ref[...].reshape(rows, L) == want
        pick = jnp.concatenate([pick, pick], axis=1)
        for t in range(IN // TILE):
            cols = slice(t * TILE, (t + 1) * TILE)
            w = weights[n, :, IN + HID + t * TILE : IN + HID + (t + 1) * TILE]
            d = jnp.dot(h2[0:rows, :], w, preferred_element_type=jnp.float32)
            out[0:rows, cols] = jnp.where(pick, d, 0.0 if initial else out[0:rows, cols])

    net(core, True)
    net(1 - core, False)


def step_kernel(positions, x1, moved1_any, mask0, mask1, *rest):
    pieces = rest[:8]
    result = rest[8]
    weights, h1, h2, out, ext, x2, moved2, moved1, sems, moved_sem = rest[9:]
    at = lax.axis_index("y") * 8 + lax.axis_index("xl") * 4 + lax.axis_index("xh") * 2 + lax.axis_index("core")
    core = lax.axis_index("core")
    base = at * 32
    lat = lax.axis_index("xh") * 2 + lax.axis_index("core")
    for k in range(8):
        for slot in range(4):
            code = positions[base + k * 4 + slot]
            row = pl.multiple_of((code % 8) * BLOCK, BLOCK)
            col = pl.multiple_of(((code // 8) % 2) * HALF, 128)
            src = pieces[k].at[pl.ds(slot * BLOCK, BLOCK), :]
            dst = weights.at[code // 16, pl.ds(row, BLOCK), pl.ds(col, HALF)]
            pltpu.make_async_copy(src, dst, sems.at[code]).start()

    arrived = pltpu.make_async_copy(moved1_any, moved1, moved_sem)
    arrived.start()

    def arrive(net, half):
        for k in range(8):
            src = pieces[0].at[pl.ds(0, BLOCK), :]
            dst = weights.at[net, pl.ds(k * BLOCK, BLOCK), pl.ds(half * HALF, HALF)]
            pltpu.make_async_copy(src, dst, sems.at[(net * 2 + half) * 8 + k]).wait()

    networks(core, x1, mask0, weights, h1, h2, out, ROWS, arrive)
    arrived.wait()

    def spread(c, carry):
        row = pl.multiple_of(c * R, R)
        for f in range(F):
            ext[c, f, 8 : 8 + R, :] = moved1[pl.ds(row, R), lanes(f)] + out[pl.ds(row, R), lanes(f)]
        return carry

    lax.fori_loop(0, WIDE, spread, 0, unroll=True)

    for c in range(C):
        for k, (at, exists) in enumerate(((7, lat > 0), (8 + R, lat < 3))):
            row = MAIN + k * C + c
            value = moved1[row : row + 1, :] + out[row : row + 1, :]
            value = jnp.where(exists, value, jnp.zeros_like(value))
            for f in range(F):
                ext[c + 1, f, at : at + 1, :] = value[:, lanes(f)]

    def second(c, carry):
        parts = own_moved(ext, c + 1)
        rs = rs_of(parts)
        row = pl.multiple_of(c * R, R)
        for f in range(F):
            moved2[pl.ds(row, R), lanes(f)] = parts[f]
            x2[pl.ds(row, R), lanes(f)] = (parts[f] * rs).astype(jnp.bfloat16)
        return carry

    lax.fori_loop(0, C, second, 0, unroll=5)
    networks(core, x2, mask1, weights, h1, h2, out, C * R, None)

    def finish(c, carry):
        row = pl.multiple_of(c * R, R)
        for f in range(F):
            result[c, f] = moved2[pl.ds(row, R), lanes(f)] + out[pl.ds(row, R), lanes(f)]
        return carry

    lax.fori_loop(0, C, finish, 0, unroll=True)


def position_table():
    out = np.zeros((32, 32), np.int32)

    def order(i, kind):
        n = ring_partner(i, 1 - kind)
        return [i, ring_partner(i, kind), n, ring_partner(n, kind)]

    for y, x, core in np.ndindex(4, 4, 2):
        codes = []
        for k, p, q in np.ndindex(8, 2, 2):
            net = core if k < 4 else 1 - core
            half, late = (k // 2) % 2, (k % 2) * 2
            if net == 0:
                bx, by = order(x, 0)[2 * half + q], order(y, half)[late + p]
            else:
                bx, by = order(x, half)[late + p], order(y, 0)[2 * half + q]
            codes.append((net * 2 + bx // 2) * 8 + by * 2 + bx % 2)
        out[device_at(y, x, core)] = codes
    return out


def vmem(n):
    return [pl.BlockSpec(memory_space=pltpu.VMEM)] * n


def steps_call():
    return pl.pallas_call(
        step_kernel,
        out_shape=jax.ShapeDtypeStruct((C, F, R, L), jnp.float32),
        in_specs=[pl.BlockSpec(memory_space=pltpu.SMEM)]
        + vmem(1)
        + [pl.BlockSpec(memory_space=pl.ANY)]
        + vmem(2)
        + [pl.BlockSpec(memory_space=pl.ANY)] * 8,
        out_specs=pl.BlockSpec(memory_space=pltpu.VMEM),
        scratch_shapes=[
            pltpu.VMEM((2, HID, 2 * HALF), jnp.bfloat16),
            pltpu.VMEM((ROWS, HID), jnp.bfloat16),
            pltpu.VMEM((ROWS, HID), jnp.bfloat16),
            pltpu.VMEM((ROWS, IN), jnp.float32),
            pltpu.VMEM((WIDE, F, 32, L), jnp.float32),
            pltpu.VMEM((C * R, IN), jnp.bfloat16),
            pltpu.VMEM((C * R, IN), jnp.float32),
            pltpu.VMEM((ROWS, IN), jnp.float32),
            pltpu.SemaphoreType.DMA((32,)),
            pltpu.SemaphoreType.DMA,
        ],
        compiler_params=pltpu.CompilerParams(vmem_limit_bytes=26 << 20),
        name="steps",
    )


def shards(fields, day_mask, w_in, w_mid, w_out):
    xh, core = lax.axis_index("xh"), lax.axis_index("core")
    joined = jnp.concatenate([w_in, w_mid, w_out], axis=2)
    block = lax.dynamic_slice(joined, (core, 0, xh * HALF), (1, 8, HALF))[0]
    pieces = gather_weights(block)

    ft = fields.transpose(1, 2, 0, 3)
    spread_masks = pl.pallas_call(
        mask_kernel,
        out_shape=(jax.ShapeDtypeStruct((C, R, L), jnp.float32),) * 2,
        in_specs=vmem(1),
        out_specs=vmem(2),
        compiler_params=pltpu.CompilerParams(vmem_limit_bytes=4 << 20),
        name="masks",
    )
    masks = spread_masks(day_mask)
    lon_n, lat_n_blocks = 128, 4
    even = lax.axis_index("z") % 2 == 0

    def as_sent(part, mask):
        return jnp.concatenate(
            [part.astype(jnp.bfloat16), mask[:, None].astype(jnp.bfloat16)], axis=1
        )

    def lon_swap(first, at_end):
        start = jnp.where(at_end, C - 2, 0)
        cols = as_sent(*(lax.dynamic_slice_in_dim(v, start, 2, 0) for v in (ft, masks[0])))
        pairs = []
        for i in range(first, lon_n + first, 2):
            pairs += [(i % lon_n, (i + 1) % lon_n), ((i + 1) % lon_n, i % lon_n)]
        return lax.ppermute(cols, LON, pairs)

    met, other = lon_swap(0, even), lon_swap(1, ~even)
    lon_w, lon_e = jnp.where(even, other, met), jnp.where(even, met, other)

    def wide(rows):
        own = as_sent(lax.optimization_barrier(ft[:, :, rows]), masks[0][:, rows])
        return jnp.concatenate([lon_w[1:, :, rows], own, lon_e[:1, :, rows]], axis=0)

    ends = range(lat_n_blocks - 1)
    lat_s = lax.ppermute(wide(slice(R - 2, R)), LAT, [(i, i + 1) for i in ends])
    lat_n = lax.ppermute(wide(slice(0, 2)), LAT, [(i + 1, i) for i in ends])

    prepare = pl.pallas_call(
        prepare_kernel,
        out_shape=(
            jax.ShapeDtypeStruct((ROWS, IN), jnp.float32),
            jax.ShapeDtypeStruct((ROWS, IN), jnp.bfloat16),
            jax.ShapeDtypeStruct((ROWS, L), jnp.float32),
        ),
        in_specs=vmem(6),
        out_specs=vmem(3),
        scratch_shapes=[
            pltpu.VMEM((C + 4, F, 32, L), jnp.float32),
            pltpu.VMEM((WIDE, F, 8, L), jnp.float32),
        ],
        compiler_params=pltpu.CompilerParams(vmem_limit_bytes=4 << 20),
        name="prepare",
    )
    moved1, x1, mask0 = prepare(ft, masks[0], lon_w, lon_e, lat_s, lat_n)

    result = steps_call()(position_table().reshape(-1), x1, moved1, mask0, masks[1], *pieces)
    return result.transpose(2, 0, 1, 3)


def solution(mesh):
    grid = Mesh(mesh.devices.reshape(4, 2, 16, 2, 2), AXES)
    in_specs = (
        P(LAT, LON, None, None),
        P(None, LAT, LON),
        P(None, LON, None),
        P(None, LON, None),
        P(None, LON, None),
    )

    return jax.shard_map(
        shards, mesh=grid, in_specs=in_specs, out_specs=P(LAT, LON, None, None), check_vma=False
    )
```

```python
import jax
import jax.numpy as jnp
import numpy as np
from jax import lax
from jax.experimental import pallas as pl
from jax.experimental.pallas import tpu as pltpu
from jax.sharding import Mesh
from jax.sharding import PartitionSpec as P

COURANT = 0.25
DIFFUSE = 0.1
EPSILON = 1e-06
AXES = ("y", "xl", "z", "xh", "core")
LON = ("y", "xl", "z")
LAT = ("xh", "core")
F, L = 6, 128
C, R = 20, 16
WIDE = C + 2
MAIN = WIDE * R
ROWS = MAIN + 2 * C + 8
IN = F * L
HID = 1024
HALF = 1280
TILE = 256
BLOCK = 128


def ring_partner(i, kind):
    if kind == 0:
        return i ^ 1
    return (i + 1) % 4 if i % 2 else (i - 1) % 4


def exchange(a, kind, first):
    pairs = []
    for y, xl, xh, core in np.ndindex(4, 2, 2, 2):
        x = xh * 2 + xl
        if (core == 0) == (first == "x"):
            px, py = ring_partner(x, kind), y
        else:
            px, py = x, ring_partner(y, kind)
        pairs.append((device_at(y, x, core), device_at(py, px, core)))
    return lax.ppermute(a, ("y", "xl", "xh", "core"), pairs)


def device_at(y, x, core):
    return ((y * 2 + x % 2) * 2 + x // 2) * 2 + core


def core_swap(a):
    return lax.ppermute(a, "core", [(0, 1), (1, 0)])


def gather_weights(block):
    z = lax.all_gather(block, "z", axis=0)
    z1 = exchange(z, 0, "x")
    a = jnp.stack([z, z1])
    b = exchange(a, 1, "x")
    a5, b5 = exchange(a, 0, "y"), exchange(b, 1, "y")
    a6, b6 = jnp.stack([a, a5]), jnp.stack([b, b5])
    a7, b7 = exchange(a6, 1, "y"), exchange(b6, 0, "y")
    ca6, cb6 = core_swap(a6), core_swap(b6)
    ca7, cb7 = core_swap(a7), core_swap(b7)
    return [p.reshape(4 * BLOCK, HALF) for p in (a6, a7, b6, b7, ca6, ca7, cb6, cb7)]


def moved_of(cen, east, west, u, v):
    north = pltpu.roll(cen, cen.shape[0] - 1, 0)
    south = pltpu.roll(cen, 1, 0)
    advected = u * (east - west) + v * (north - south)
    smoothed = east + west + north + south - 4.0 * cen
    return cen - COURANT * advected + DIFFUSE * smoothed


def column_moved(ext, c):
    cen = [ext[c, f] for f in range(F)]
    return [moved_of(cen[f], ext[c + 1, f], ext[c - 1, f], cen[0], cen[1]) for f in range(F)]


def own_moved(ext, c):
    rows = slice(8, 8 + R)
    cen = [ext[c, f, rows, :] for f in range(F)]
    u, v = COURANT * cen[0], COURANT * cen[1]
    out = []
    for f in range(F):
        east, west = ext[c + 1, f, rows, :], ext[c - 1, f, rows, :]
        north, south = ext[c, f, 9 : 9 + R, :], ext[c, f, 7 : 7 + R, :]
        advected = u * (east - west) + v * (north - south)
        smoothed = (east + west) + (north + south) - 4.0 * cen[f]
        out.append(cen[f] - advected + DIFFUSE * smoothed)
    return out


def rs_of(parts):
    ss = parts[0] * parts[0]
    for p in parts[1:]:
        ss = ss + p * p
    return lax.rsqrt(jnp.sum(ss, axis=-1, keepdims=True) * (1.0 / IN) + EPSILON)


def lanes(f):
    return slice(f * L, (f + 1) * L)


def mask_kernel(days, first, second):
    for out, step in ((first, 0), (second, 1)):
        m = days[step].astype(jnp.float32)
        for c in range(C):
            out[c] = jnp.broadcast_to(m[:, c : c + 1], (R, L))


def prepare_kernel(ft, mask, lon_w, lon_e, lat_s, lat_n, moved, normed, mk, ext, edge):
    moved[MAIN:, :] = jnp.zeros((ROWS - MAIN, IN), jnp.float32)
    mk[MAIN:, :] = jnp.zeros((ROWS - MAIN, L), jnp.float32)

    def own(c, carry):
        for f in range(F):
            ext[c + 2, f, 8 : 8 + R, :] = ft[c, f]
        row = pl.multiple_of((c + 1) * R, R)
        mk[pl.ds(row, R), :] = mask[c]
        return carry

    lax.fori_loop(0, C, own, 0)
    for c in range(2):
        for f in range(F):
            ext[c, f, 8 : 8 + R, :] = lon_w[c, f].astype(jnp.float32)
            ext[C + 2 + c, f, 8 : 8 + R, :] = lon_e[c, f].astype(jnp.float32)
    mk[0:R, :] = lon_w[1, F].astype(jnp.float32)
    mk[MAIN - R : MAIN, :] = lon_e[0, F].astype(jnp.float32)

    def sides(c, carry):
        for f in range(F):
            ext[c + 1, f, 6:8, :] = lat_s[c, f].astype(jnp.float32)
            ext[c + 1, f, 8 + R : 10 + R, :] = lat_n[c, f].astype(jnp.float32)
        return carry

    lax.fori_loop(0, WIDE, sides, 0)

    def step(c, carry):
        parts = column_moved(ext, c + 1)
        rs = rs_of(parts)
        row = pl.multiple_of(c * R, R)
        for f in range(F):
            moved[pl.ds(row, R), lanes(f)] = parts[f][8 : 8 + R]
            normed[pl.ds(row, R), lanes(f)] = (parts[f] * rs)[8 : 8 + R].astype(jnp.bfloat16)

        for f in range(F):
            edge[c, f, 0:1, :] = parts[f][7:8]
            edge[c, f, 1:2, :] = parts[f][8 + R : 9 + R]
        return carry

    lax.fori_loop(0, WIDE, step, 0)
    for c in range(C):
        for k, side in enumerate((lat_s, lat_n)):
            row = MAIN + k * C + c
            for f in range(F):
                moved[row : row + 1, lanes(f)] = edge[c + 1, f, k : k + 1, :]
            mk[row : row + 1, :] = side[c + 1, F].astype(jnp.float32)[1 - k : 2 - k]
    tail = [moved[MAIN:, lanes(f)] for f in range(F)]
    rs = rs_of(tail)
    for f in range(F):
        normed[MAIN:, lanes(f)] = (tail[f] * rs).astype(jnp.bfloat16)


def silu(t):
    half = 0.5 * t
    return (half + half * jnp.tanh(half)).astype(jnp.bfloat16)


def network(n, x, mask_ref, weights, h1, h2, out, before, rows, arrive):
    want = (1 - n).astype(jnp.float32)
    arrive(0)
    for t in range(HID // TILE):
        w = weights[t * TILE : (t + 1) * TILE, 0:IN]
        d = lax.dot_general(x[...], w, (((1,), (1,)), ((), ())), preferred_element_type=jnp.float32)
        h1[0:rows, t * TILE : (t + 1) * TILE] = silu(d)
    arrive(1)
    for t in range(HID // TILE):
        w = weights[:, IN + t * TILE : IN + (t + 1) * TILE]
        d = jnp.dot(h1[0:rows, :], w, preferred_element_type=jnp.float32)
        h2[0:rows, t * TILE : (t + 1) * TILE] = silu(d)
    pick = mask_ref[...].reshape(rows, L) == want
    pick = jnp.concatenate([pick, pick], axis=1)
    for t in range(IN // TILE):
        cols = slice(t * TILE, (t + 1) * TILE)
        w = weights[:, IN + HID + t * TILE : IN + HID + (t + 1) * TILE]
        d = jnp.dot(h2[0:rows, :], w, preferred_element_type=jnp.float32)
        out[0:rows, cols] = jnp.where(pick, d, 0.0 if before is None else before[0:rows, cols])


def here():
    xl, xh, core = (lax.axis_index(a) for a in ("xl", "xh", "core"))
    return (lax.axis_index("y") * 8 + xl * 4 + xh * 2 + core) * 32, core, xh * 2 + core


def place(positions, base, pieces, weights, sems):
    for k in range(4):
        for slot in range(4):
            code = positions[base + k * 4 + slot] % 16
            row = pl.multiple_of((code % 8) * BLOCK, BLOCK)
            col = pl.multiple_of((code // 8) * HALF, 128)
            src = pieces[k].at[pl.ds(slot * BLOCK, BLOCK), :]
            dst = weights.at[pl.ds(row, BLOCK), pl.ds(col, HALF)]
            pltpu.make_async_copy(src, dst, sems.at[code]).start()

    def arrive(half):
        for k in range(8):
            src = pieces[0].at[pl.ds(0, BLOCK), :]
            dst = weights.at[pl.ds(k * BLOCK, BLOCK), pl.ds(half * HALF, HALF)]
            pltpu.make_async_copy(src, dst, sems.at[half * 8 + k]).wait()

    return arrive


def own_kernel(positions, x1, mask0, a6, a7, b6, b7, out, own, h1, h2, sems):
    base, core, _ = here()
    arrive = place(positions, base, (a6, a7, b6, b7), own, sems)
    network(core, x1, mask0, own, h1, h2, out, None, ROWS, arrive)


def step_kernel(positions, x1, moved1_any, mask0, mask1, out1, own, *rest):
    pieces = rest[:4]
    result = rest[4]
    other, h1, h2, out, ext, x2, moved2, moved1, sems, moved_sem = rest[5:]
    base, core, lat = here()
    arrive = place(positions, base + 16, pieces, other, sems)
    arrived = pltpu.make_async_copy(moved1_any, moved1, moved_sem)
    arrived.start()

    network(1 - core, x1, mask0, other, h1, h2, out, out1, ROWS, arrive)
    arrived.wait()

    def spread(c, carry):
        row = pl.multiple_of(c * R, R)
        for f in range(F):
            ext[c, f, 8 : 8 + R, :] = moved1[pl.ds(row, R), lanes(f)] + out[pl.ds(row, R), lanes(f)]
        return carry

    lax.fori_loop(0, WIDE, spread, 0, unroll=True)

    for c in range(C):
        for k, (at, exists) in enumerate(((7, lat > 0), (8 + R, lat < 3))):
            row = MAIN + k * C + c
            value = moved1[row : row + 1, :] + out[row : row + 1, :]
            value = jnp.where(exists, value, jnp.zeros_like(value))
            for f in range(F):
                ext[c + 1, f, at : at + 1, :] = value[:, lanes(f)]

    def second(c, carry):
        parts = own_moved(ext, c + 1)
        rs = rs_of(parts)
        row = pl.multiple_of(c * R, R)
        for f in range(F):
            moved2[pl.ds(row, R), lanes(f)] = parts[f]
            x2[pl.ds(row, R), lanes(f)] = (parts[f] * rs).astype(jnp.bfloat16)
        return carry

    lax.fori_loop(0, C, second, 0, unroll=5)
    ready = lambda half: None
    network(core, x2, mask1, own, h1, h2, out, None, C * R, ready)
    network(1 - core, x2, mask1, other, h1, h2, out, out, C * R, ready)

    def finish(c, carry):
        row = pl.multiple_of(c * R, R)
        for f in range(F):
            result[c, f] = moved2[pl.ds(row, R), lanes(f)] + out[pl.ds(row, R), lanes(f)]
        return carry

    lax.fori_loop(0, C, finish, 0, unroll=True)


def position_table():
    out = np.zeros((32, 32), np.int32)

    def order(i, kind):
        n = ring_partner(i, 1 - kind)
        return [i, ring_partner(i, kind), n, ring_partner(n, kind)]

    for y, x, core in np.ndindex(4, 4, 2):
        codes = []
        for k, p, q in np.ndindex(8, 2, 2):
            net = core if k < 4 else 1 - core
            half, late = (k // 2) % 2, (k % 2) * 2
            if net == 0:
                bx, by = order(x, 0)[2 * half + q], order(y, half)[late + p]
            else:
                bx, by = order(x, half)[late + p], order(y, 0)[2 * half + q]
            codes.append((net * 2 + bx // 2) * 8 + by * 2 + bx % 2)
        out[device_at(y, x, core)] = codes
    return out


def vmem(n):
    return [pl.BlockSpec(memory_space=pltpu.VMEM)] * n


SMEM_SPEC = [pl.BlockSpec(memory_space=pltpu.SMEM)]
ANY_SPEC = [pl.BlockSpec(memory_space=pl.ANY)]


def own_call():
    return pl.pallas_call(
        own_kernel,
        out_shape=(
            jax.ShapeDtypeStruct((ROWS, IN), jnp.float32),
            jax.ShapeDtypeStruct((HID, 2 * HALF), jnp.bfloat16),
        ),
        in_specs=SMEM_SPEC + vmem(2) + ANY_SPEC * 4,
        out_specs=vmem(2),
        scratch_shapes=[
            pltpu.VMEM((ROWS, HID), jnp.bfloat16),
            pltpu.VMEM((ROWS, HID), jnp.bfloat16),
            pltpu.SemaphoreType.DMA((16,)),
        ],
        compiler_params=pltpu.CompilerParams(vmem_limit_bytes=14 << 20),
        name="own",
    )


def steps_call():
    return pl.pallas_call(
        step_kernel,
        out_shape=jax.ShapeDtypeStruct((C, F, R, L), jnp.float32),
        in_specs=SMEM_SPEC + vmem(1) + ANY_SPEC + vmem(4) + ANY_SPEC * 4,
        out_specs=pl.BlockSpec(memory_space=pltpu.VMEM),
        scratch_shapes=[
            pltpu.VMEM((HID, 2 * HALF), jnp.bfloat16),
            pltpu.VMEM((ROWS, HID), jnp.bfloat16),
            pltpu.VMEM((ROWS, HID), jnp.bfloat16),
            pltpu.VMEM((ROWS, IN), jnp.float32),
            pltpu.VMEM((WIDE, F, 32, L), jnp.float32),
            pltpu.VMEM((C * R, IN), jnp.bfloat16),
            pltpu.VMEM((C * R, IN), jnp.float32),
            pltpu.VMEM((ROWS, IN), jnp.float32),
            pltpu.SemaphoreType.DMA((16,)),
            pltpu.SemaphoreType.DMA,
        ],
        compiler_params=pltpu.CompilerParams(vmem_limit_bytes=26 << 20),
        name="steps",
    )


def shards(fields, day_mask, w_in, w_mid, w_out):
    xh, core = lax.axis_index("xh"), lax.axis_index("core")
    joined = jnp.concatenate([w_in, w_mid, w_out], axis=2)
    block = lax.dynamic_slice(joined, (core, 0, xh * HALF), (1, 8, HALF))[0]
    pieces = gather_weights(block)

    ft = fields.transpose(1, 2, 0, 3)
    spread_masks = pl.pallas_call(
        mask_kernel,
        out_shape=(jax.ShapeDtypeStruct((C, R, L), jnp.float32),) * 2,
        in_specs=vmem(1),
        out_specs=vmem(2),
        compiler_params=pltpu.CompilerParams(vmem_limit_bytes=4 << 20),
        name="masks",
    )
    masks = spread_masks(day_mask)
    lon_n, lat_n_blocks = 128, 4
    even = lax.axis_index("z") % 2 == 0

    def as_sent(part, mask):
        return jnp.concatenate(
            [part.astype(jnp.bfloat16), mask[:, None].astype(jnp.bfloat16)], axis=1
        )

    def lon_swap(first, at_end):
        start = jnp.where(at_end, C - 2, 0)
        cols = as_sent(*(lax.dynamic_slice_in_dim(v, start, 2, 0) for v in (ft, masks[0])))
        pairs = []
        for i in range(first, lon_n + first, 2):
            pairs += [(i % lon_n, (i + 1) % lon_n), ((i + 1) % lon_n, i % lon_n)]
        return lax.ppermute(cols, LON, pairs)

    met, other = lon_swap(0, even), lon_swap(1, ~even)
    lon_w, lon_e = jnp.where(even, other, met), jnp.where(even, met, other)

    def wide(rows):
        own = as_sent(lax.optimization_barrier(ft[:, :, rows]), masks[0][:, rows])
        return jnp.concatenate([lon_w[1:, :, rows], own, lon_e[:1, :, rows]], axis=0)

    ends = range(lat_n_blocks - 1)
    lat_s = lax.ppermute(wide(slice(R - 2, R)), LAT, [(i, i + 1) for i in ends])
    lat_n = lax.ppermute(wide(slice(0, 2)), LAT, [(i + 1, i) for i in ends])

    prepare = pl.pallas_call(
        prepare_kernel,
        out_shape=(
            jax.ShapeDtypeStruct((ROWS, IN), jnp.float32),
            jax.ShapeDtypeStruct((ROWS, IN), jnp.bfloat16),
            jax.ShapeDtypeStruct((ROWS, L), jnp.float32),
        ),
        in_specs=vmem(6),
        out_specs=vmem(3),
        scratch_shapes=[
            pltpu.VMEM((C + 4, F, 32, L), jnp.float32),
            pltpu.VMEM((WIDE, F, 8, L), jnp.float32),
        ],
        compiler_params=pltpu.CompilerParams(vmem_limit_bytes=4 << 20),
        name="prepare",
    )
    moved1, x1, mask0 = prepare(ft, masks[0], lon_w, lon_e, lat_s, lat_n)

    positions = position_table().reshape(-1)
    out1, own = own_call()(positions, x1, mask0, *pieces[:4])
    result = steps_call()(positions, x1, moved1, mask0, masks[1], out1, own, *pieces[4:])
    return result.transpose(2, 0, 1, 3)


def solution(mesh):
    grid = Mesh(mesh.devices.reshape(4, 2, 16, 2, 2), AXES)
    in_specs = (
        P(LAT, LON, None, None),
        P(None, LAT, LON),
        P(None, LON, None),
        P(None, LON, None),
        P(None, LON, None),
    )

    return jax.shard_map(
        shards, mesh=grid, in_specs=in_specs, out_specs=P(LAT, LON, None, None), check_vma=False
    )
```
